256 devices in a mesh: region: 16 (over y, x), band: 16 (over z, core).
Axes of the slice: x: 4, y: 4, z: 8, core: 2. Of those that a mesh axis runs over, the one named last changes fastest.
Arguments:
- adjoint_in: float32 [128, 256, 2048], P(None, 'band', 'region'), may hold values from -6 to 6
- courant_y: float32 [128, 256, 2048], P(None, 'band', 'region'), may hold values from -0.45 to 0.45
- courant_x: float32 [128, 256, 2048], P('band', None, 'region'), may hold values from -0.45 to 0.45
- diffusion_inverse: float32 [256, 128, 128], P('band')
- conv_weight: float32 [256, 2048], P('band', 'region'), may hold values from 0.05 to 0.9
- cloud_base: int32 [256, 2048], P('band', 'region'), may hold values from 0 to 63
- cloud_top: int32 [256, 2048], P('band', 'region'), may hold values from 1 to 126, as said below
- sound_count: int32 [16, 256], P('region', 'band'), may hold values from 0 to 64, as said below
- xco2_adjoint: float32 [16, 256, 64], P('region', 'band'), may hold values from -6 to 6
- kernel: float32 [16, 256, 64, 128], P('region', 'band'), may hold values from 0.25 to 4
- sound_cols: int32 [16, 256, 64], P('region', 'band'), may hold values from 0 to 2047
Outputs:
- adjoint_out: float32 [128, 256, 2048], P('band', None, 'region')
The draws below stay inside these ranges and needn't reach their ends.
Inputs may be any that keep to these rules, and one draw needn't show every extreme that they name: `sound_count`: in every region one destination band receives 64 live slots from every source band. `sound_cols`: several slots may name the same column; the column is the latitude row within the band times 128 plus the longitude within the region. cloud_top > cloud_base in every column.
All inputs are finite; a program needn't handle non-finite values.
Results may differ from the reference program's by a relative error of at most 0.00014.
Values sent between devices are 32-bit elements; how exact they have to be, the bound alone decides.
No kernel may reach another device: no remote copies, remote signals or barrier semaphores. Data moves between devices by JAX's collectives and lax.ppermute only.
A program may use at most 64 MiB of HBM per device.

```python
import math
import jax
import jax.numpy as jnp
from jax import lax

LEV = 128
LAT_DEV = 16
LON_DEV = 128
SLOTS = 64
YSTEPS = 2
XSTEPS = 4
REGIONS = 16
BANDS = 16
LAT = 256
LON = 2048


def cloud_levels(key):
    key_base, key_depth = jax.random.split(key)
    lowest = jax.random.randint(key_base, (LAT, LON), 0, LEV // 2, dtype=jnp.int32)
    cloud_depth = jax.random.randint(key_depth, (LAT, LON), 1, LEV // 2, dtype=jnp.int32)
    return (lowest, lowest + cloud_depth)


def draw_cloud_base(key, part):
    return cloud_levels(jax.random.fold_in(key, 17))[0]


def draw_cloud_top(key, part):
    return cloud_levels(jax.random.fold_in(key, 17))[1]


def draw_sound_count(key, part):
    key_count, key_busy = jax.random.split(jax.random.fold_in(key, 29))
    counts = jax.random.randint(key_count, (REGIONS, BANDS, BANDS), 0, SLOTS + 1, dtype=jnp.int32)
    busiest = jax.random.randint(key_busy, (REGIONS, 1, 1), 0, BANDS, dtype=jnp.int32)
    dest_band = jnp.arange(BANDS, dtype=jnp.int32)[None, None, :]
    counts = jnp.where(dest_band == busiest, SLOTS, counts)
    return counts.reshape(REGIONS, BANDS * BANDS)


def draw_diffusion_inverse(key, part):
    spread_part = jax.random.normal(key, (LAT, LEV, LEV), jnp.float32) * (0.5 / math.sqrt(LEV))
    levels = jnp.arange(LEV, dtype=jnp.int32)
    identity = (levels[:, None] == levels[None, :]).astype(jnp.float32)
    return identity[None] + spread_part


def plant(entries, stream_key, low, top_value):
    shape = entries.shape
    place = [jax.random.randint(jax.random.fold_in(stream_key, axis), (), 0, shape[axis]) for axis in range(len(shape))]
    entries = entries.at[tuple(place)].set(low)
    longest = shape.index(max(shape))
    place[longest] = (place[longest] + 1) % shape[longest]
    return entries.at[tuple(place)].set(top_value)


def steps_of(own_key, extent, cuts, low, largest):
    level, own = 1.0, jax.random.fold_in(own_key, 6)
    for dim, parts in cuts:
        steps = jnp.exp(jax.random.uniform(jax.random.fold_in(own, dim), (parts,), jnp.float32, low / len(cuts), largest / len(cuts)))
        level = level * jnp.repeat(steps, extent[dim] // parts).reshape([-1 if axis == dim else 1 for axis in range(len(extent))])
    return level


def noise(key, extent, width, most, pieces=(), kind=jnp.bfloat16):
    drawn = jax.random.normal(key, extent, jnp.float32) * width
    if len(pieces) > 0:
        drawn = steps_of(key, extent, pieces, -0.22, 0.18) * drawn
    return jnp.clip(drawn, min=-most, max=most).astype(kind)


def setup_inputs(seed: int = 0) -> dict:
    keys = jax.random.split(jax.random.key(seed), 12)
    return {
        "adjoint_in": noise(keys[0], (LEV, LAT, LON), 1.0, 6.0, ((1, 16), (2, 16)), jnp.float32),
        "courant_y": jnp.clip(jax.random.uniform(keys[1], (LEV, LAT, LON), jnp.float32, -0.45, 0.45) * steps_of(keys[1], (LEV, LAT, LON), ((1, 16), (2, 16)), -0.4, 0.0), -0.45, 0.45),
        "courant_x": jnp.clip(jax.random.uniform(keys[2], (LEV, LAT, LON), jnp.float32, -0.45, 0.45) * steps_of(keys[2], (LEV, LAT, LON), ((0, 16), (2, 16)), -0.4, 0.0), -0.45, 0.45),
        "diffusion_inverse": draw_diffusion_inverse(jax.random.fold_in(keys[11], 71), 0),
        "conv_weight": jnp.clip(jnp.exp(math.log(0.9) - 2.8903717 * jax.random.uniform(keys[4], (LAT, LON), jnp.float32) ** steps_of(keys[4], (LAT, LON), ((0, 16), (1, 16)), -0.2, 0.2)), 0.05, 0.9),
        "cloud_base": draw_cloud_base(jax.random.fold_in(keys[11], 71), 0),
        "cloud_top": draw_cloud_top(jax.random.fold_in(keys[11], 71), 0),
        "sound_count": draw_sound_count(jax.random.fold_in(keys[11], 71), 0),
        "xco2_adjoint": noise(keys[8], (REGIONS, BANDS * BANDS, SLOTS), 1.0, 6.0, ((0, 16), (1, 16)), jnp.float32),
        "kernel": jnp.clip(jnp.exp(math.log(4.0) - 2.7725887 * jax.random.uniform(keys[9], (REGIONS, BANDS * BANDS, SLOTS, LEV), jnp.float32) ** steps_of(keys[9], (REGIONS, BANDS * BANDS, SLOTS, LEV), ((0, 16), (1, 16)), -0.2, 0.2)), 0.25, 4.0),
        "sound_cols": plant(jax.random.randint(keys[10], (REGIONS, BANDS * BANDS, SLOTS), 0, LAT_DEV * LON_DEV), jax.random.fold_in(keys[10], 1), 0, (LAT_DEV * LON_DEV) - 1).astype(jnp.int32),
    }


def take_next(field, dim):
    kept_part = lax.slice_in_dim(field, 1, field.shape[dim], axis=dim)
    zero_edge = jnp.zeros_like(lax.slice_in_dim(field, 0, 1, axis=dim))
    return jnp.concatenate([kept_part, zero_edge], axis=dim)


def take_prev(field, dim):
    kept_part = lax.slice_in_dim(field, 0, field.shape[dim] - 1, axis=dim)
    zero_edge = jnp.zeros_like(lax.slice_in_dim(field, 0, 1, axis=dim))
    return jnp.concatenate([zero_edge, kept_part], axis=dim)


def advect_sweep(tracer, courant, dim):
    outflow_up = jnp.maximum(courant, 0.0)
    lower_prev = take_prev(jnp.minimum(courant, 0.0), dim)
    return (1.0 - outflow_up + lower_prev) * tracer + outflow_up * take_next(tracer, dim) - lower_prev * take_prev(tracer, dim)


def periodic_sweep(tracer, courant):
    outflow_up = jnp.maximum(courant, 0.0)
    lower_prev = jnp.roll(jnp.minimum(courant, 0.0), 1, axis=2)
    return (1.0 - outflow_up + lower_prev) * tracer + outflow_up * jnp.roll(tracer, -1, axis=2) - lower_prev * jnp.roll(tracer, 1, axis=2)


def convect(field, cloud_base, cloud_top, conv_weight):
    levels = jnp.arange(field.shape[0], dtype=jnp.int32)[:, None, None]
    inside = ((levels >= cloud_base[None]) & (levels <= cloud_top[None])).astype(field.dtype)
    cloud_depth = (cloud_top - cloud_base + 1).astype(field.dtype)
    column_mean = jnp.sum(inside * field, axis=0) / cloud_depth
    return field + conv_weight[None] * inside * (column_mean[None] - field)


def reference(adjoint_in, courant_y, courant_x, diffusion_inverse, conv_weight, cloud_base, cloud_top, sound_count, xco2_adjoint, kernel, sound_cols):
    slot_index = jnp.arange(SLOTS, dtype=jnp.int32)
    live_slot = slot_index[None, None, :] < sound_count[:, :, None]
    partial_value = jnp.where(live_slot, xco2_adjoint, jnp.zeros_like(xco2_adjoint))[..., None] * kernel
    partial_value = partial_value.reshape(REGIONS, BANDS, BANDS, SLOTS, LEV).transpose(0, 2, 1, 3, 4)
    slot_cols = sound_cols.reshape(REGIONS, BANDS, BANDS, SLOTS)
    region_index = jnp.arange(REGIONS, dtype=jnp.int32)[:, None, None, None]
    dest_band = jnp.arange(BANDS, dtype=jnp.int32)[None, :, None, None]
    lat_index = dest_band * LAT_DEV + slot_cols // LON_DEV
    lon_index = region_index * LON_DEV + slot_cols % LON_DEV
    flat_cols = (lat_index * LON + lon_index).reshape(-1).astype(jnp.int32)
    column = adjoint_in.reshape(LEV, LAT * LON)
    forced = column.at[:, flat_cols].add(partial_value.reshape(-1, LEV).T).reshape(LEV, LAT, LON)
    convected = convect(forced, cloud_base, cloud_top, conv_weight)
    tracer = jnp.einsum("jlk,lji->kji", diffusion_inverse, convected, precision=lax.Precision.HIGHEST)
    rows = jnp.arange(LAT, dtype=jnp.int32)[None, :, None]
    courant_eff = jnp.where(rows < LAT - 1, courant_y, jnp.zeros_like(courant_y))
    for substep in range(YSTEPS):
        tracer = advect_sweep(tracer, courant_eff, 1)
    for substep in range(XSTEPS):
        tracer = periodic_sweep(tracer, courant_x)
    return tracer
```

```python
import jax
import jax.numpy as jnp
from jax import lax
from jax.sharding import PartitionSpec as P

YSTEPS = 2
XSTEPS = 4


def neighbours(head, tail, axis):
    count = lax.axis_size(axis)
    from_prev = lax.ppermute(tail, axis, [(i, (i + 1) % count) for i in range(count)])
    from_next = lax.ppermute(head, axis, [((i + 1) % count, i) for i in range(count)])
    return from_prev, from_next


def shrink_sweep(tracer, courant, dim):
    n = tracer.shape[dim]

    def cut(field, lo, hi):
        return lax.slice_in_dim(field, lo, hi, axis=dim)

    up = jnp.maximum(cut(courant, 1, n - 1), 0.0)
    low = jnp.minimum(cut(courant, 0, n - 2), 0.0)
    return (
        (1.0 - up + low) * cut(tracer, 1, n - 1)
        + up * cut(tracer, 2, n)
        - low * cut(tracer, 0, n - 2)
    )


def vertical_mix(field, diffusion_inverse, conv_weight, cloud_base, cloud_top):
    levels = jnp.arange(field.shape[0], dtype=jnp.int32)[:, None, None]
    inside = ((levels >= cloud_base[None]) & (levels <= cloud_top[None])).astype(jnp.float32)
    cloud_depth = (cloud_top - cloud_base + 1).astype(jnp.float32)
    column_mean = jnp.sum(inside * field, axis=0) / cloud_depth
    convected = field + conv_weight[None] * inside * (column_mean[None] - field)
    return jnp.einsum("jlk,lji->kji", diffusion_inverse, convected, precision=lax.Precision.HIGHEST)


def per_device(
    adjoint_in,
    courant_y,
    courant_x,
    diffusion_inverse,
    conv_weight,
    cloud_base,
    cloud_top,
    sound_count,
    xco2_adjoint,
    kernel,
    sound_cols,
):
    levels, lat_rows, lon_cells = adjoint_in.shape
    slot_count = kernel.shape[2]
    slot_index = jnp.arange(slot_count, dtype=jnp.int32)
    live_slot = slot_index[None, None, :] < sound_count[:, :, None]
    partial_value = jnp.where(live_slot, xco2_adjoint, 0.0)[..., None] * kernel
    arrived = lax.all_to_all(partial_value, "band", split_axis=1, concat_axis=1, tiled=True)
    flat_cols = sound_cols.reshape(-1)
    update = arrived.reshape(-1, levels).T
    column = adjoint_in.reshape(levels, lat_rows * lon_cells)
    forced = column.at[:, flat_cols].add(update).reshape(adjoint_in.shape)
    mixed = vertical_mix(forced, diffusion_inverse, conv_weight, cloud_base, cloud_top)

    band = lax.axis_index("band")
    last_band = lax.axis_size("band") - 1
    cy_prev, cy_next = neighbours(courant_y[:, :2], courant_y[:, -2:], "band")
    cy = jnp.concatenate([cy_prev, courant_y, cy_next], axis=1)
    row = jnp.arange(lat_rows + 4, dtype=jnp.int32) - 2 + band * lat_rows
    n_lat = lat_rows * (last_band + 1)
    cy = jnp.where(((row >= 0) & (row < n_lat - 1))[None, :, None], cy, 0.0)
    m_prev, m_next = neighbours(mixed[:, :2], mixed[:, -2:], "band")
    m_prev = jnp.where(band > 0, m_prev, 0.0)
    m_next = jnp.where(band < last_band, m_next, 0.0)
    tracer = jnp.concatenate([m_prev, mixed, m_next], axis=1)
    tracer = shrink_sweep(tracer, cy, 1)
    tracer = shrink_sweep(tracer, cy[:, 1:-1], 1)

    slab = lax.all_to_all(tracer, "band", split_axis=0, concat_axis=1, tiled=True)
    cx_prev, cx_next = neighbours(courant_x[:, :, :XSTEPS], courant_x[:, :, -XSTEPS:], "region")
    cx = jnp.concatenate([cx_prev, courant_x, cx_next], axis=2)
    s_prev, s_next = neighbours(slab[:, :, :XSTEPS], slab[:, :, -XSTEPS:], "region")
    result = jnp.concatenate([s_prev, slab, s_next], axis=2)
    for step in range(XSTEPS):
        result = shrink_sweep(result, cx[:, :, step : cx.shape[2] - step], 2)
    return result


def solution(mesh):
    in_specs = (
        P(None, "band", "region"),
        P(None, "band", "region"),
        P("band", None, "region"),
        P("band", None, None),
        P("band", "region"),
        P("band", "region"),
        P("band", "region"),
        P("region", "band"),
        P("region", "band", None),
        P("region", "band", None, None),
        P("region", "band", None),
    )
    out_specs = P("band", None, "region")
    return jax.shard_map(
        per_device, mesh=mesh, in_specs=in_specs, out_specs=out_specs, check_vma=False
    )
```

```python
import jax
import jax.numpy as jnp
from jax import lax
from jax.experimental import pallas as pl
from jax.experimental.pallas import tpu as pltpu
from jax.sharding import PartitionSpec as P


XSTEPS = 4
LEV = 128
ROWS = 16
LON = 128
BANDS = 16
SLAB = 8
STRIP = 16
HALVES = 2
GROUP = 4
CHUNK = 4
WIDE = ROWS + 4

f32 = jnp.float32
bf16 = jnp.bfloat16


def split(x):
    hi = x.astype(bf16)
    return hi, (x - hi.astype(f32)).astype(bf16)


def lane_iota(shape):
    return lax.broadcasted_iota(jnp.int32, shape, len(shape) - 1)


def turned(x, shift):
    shift %= LON
    return pltpu.roll(x, shift, x.ndim - 1) if shift else x


def pack_strips(tile_of):
    left, right = [], []
    for half in range(HALVES):
        west = east = None
        for g in range(ROWS // HALVES):
            tile = tile_of(half * (ROWS // HALVES) + g)
            here = lane_iota(tile.shape) // STRIP == g
            to_west = turned(tile, STRIP * g + XSTEPS)
            to_east = turned(tile, STRIP * g + STRIP - XSTEPS)
            west = to_west if west is None else jnp.where(here, to_west, west)
            east = to_east if east is None else jnp.where(here, to_east, east)
        left.append(west)
        right.append(east)
    return left, right


def scale_kernel(count_hbm, value_hbm, kern_hbm, out_hbm, count, value, kern, sem, kern_sem, out_sem):
    small = [
        pltpu.make_async_copy(count_hbm, count, sem.at[0]),
        pltpu.make_async_copy(value_hbm, value, sem.at[1]),
    ]
    spans = [pl.ds(c * GROUP, GROUP) for c in range(BANDS // GROUP)]
    loads = [pltpu.make_async_copy(kern_hbm.at[0, spans[c]], kern.at[spans[c]], kern_sem.at[c]) for c in range(len(spans))]
    stores = [pltpu.make_async_copy(kern.at[spans[c]], out_hbm.at[spans[c]], out_sem.at[c]) for c in range(len(spans))]
    for copy in small + loads:
        copy.start()
    for copy in small:
        copy.wait()
    factor = value[0].T
    live = lax.broadcasted_iota(jnp.int32, factor.shape, 0) < count[...]
    factor = jnp.where(live, factor, 0.0)
    for c in range(len(spans)):
        loads[c].wait()
        for band in range(c * GROUP, c * GROUP + GROUP):
            kern[band] = kern[band] * factor[:, band : band + 1]
        stores[c].start()
    for copy in stores:
        copy.wait()


def prepare_kernel(field_hbm, cy_hbm, diff_hbm, field_out, cy_out, diff_out, field, cy, diff, parts, sem, out_sem):
    loads = [
        pltpu.make_async_copy(diff_hbm, diff, sem.at[0]),
        pltpu.make_async_copy(field_hbm, field, sem.at[1]),
        pltpu.make_async_copy(cy_hbm, cy, sem.at[2]),
    ]
    for copy in loads:
        copy.start()
    loads[0].wait()
    for row in range(ROWS):
        hi, lo = split(diff[row].T)
        parts[row, 0] = hi
        parts[row, 1] = lo
    store = pltpu.make_async_copy(parts, diff_out, out_sem)
    store.start()
    loads[1].wait()
    for row in range(ROWS):
        field_out[row] = field[:, row, :]
    loads[2].wait()
    for row in range(ROWS):
        cy_out[row] = cy[:, row, :]
    store.wait()


def faces_kernel(cx_ref, cx_out, left_out, right_out):
    def source(s, carry):
        def tile_of(row):
            tile = cx_ref[:, pl.ds(s * ROWS + row, 1), :].reshape(SLAB, LON)
            cx_out[s * ROWS + row] = tile
            return tile

        left, right = pack_strips(tile_of)
        for half in range(HALVES):
            left_out[s, half] = left[half]
            right_out[s, half] = right[half]
        return carry

    lax.fori_loop(0, BANDS, source, 0)


def fill_halo(left, right, west, east):
    spot = lane_iota(left.shape) % STRIP
    left = jnp.where(spot < XSTEPS, turned(west, XSTEPS - STRIP + XSTEPS), left)
    right = jnp.where(spot >= STRIP - XSTEPS, turned(east, STRIP - 2 * XSTEPS), right)
    return left, right


def stencil_of(courant):
    up = jnp.maximum(courant, 0.0)
    low = turned(jnp.minimum(courant, 0.0), 1)
    return 1.0 - up + low, up, low


def zonal_sweep(value, keep, up, low):
    return keep * value + up * turned(value, -1) - low * turned(value, 1)


def sides_kernel(left_ref, right_ref, west_ref, east_ref, coef_out):
    def source(s, carry):
        for half in range(HALVES):
            strips = fill_halo(left_ref[s, half], right_ref[s, half], west_ref[s, half], east_ref[s, half])
            for side in range(2):
                for k, value in enumerate(stencil_of(strips[side])):
                    coef_out[s, half, side, k] = value
        return carry

    lax.fori_loop(0, BANDS, source, 0)


def mix_kernel(
    kern_ref, cols_ref, field_ref, cy_ref, before_ref, after_ref, diff_hbm, conv_hbm, base_hbm, top_hbm,
    block_out,
    parts, onehot, mixed, once, diff_buf, conv_ref, base_ref, top_ref, diff_sem, sem,
):
    def diff_copy(g):
        span = pl.ds(g * GROUP, GROUP)
        return pltpu.make_async_copy(diff_hbm.at[span], diff_buf.at[span], diff_sem.at[g])

    small = [
        pltpu.make_async_copy(conv_hbm, conv_ref, sem.at[0]),
        pltpu.make_async_copy(base_hbm, base_ref, sem.at[1]),
        pltpu.make_async_copy(top_hbm, top_ref, sem.at[2]),
    ]
    for copy in small + [diff_copy(g) for g in range(ROWS // GROUP)]:
        copy.start()
    for c in range(8):
        span = slice(c * 128, c * 128 + 128)
        hi, lo = split(kern_ref[span, :])
        parts[span, :LEV] = hi
        parts[span, LEV:] = lo

    for copy in small:
        copy.wait()
    level = lax.broadcasted_iota(jnp.int32, (LEV, LON), 0)

    def group(g, carry):
        cols = cols_ref[...] - g * (GROUP * LON)
        for r in range(0, GROUP * LON, 32):
            cell = lax.broadcasted_iota(jnp.int32, (32, cols.shape[1]), 0) + r
            onehot[pl.ds(r, 32), :] = jnp.where(cell == cols, 1.0, 0.0).astype(bf16)
        both = jnp.dot(onehot[...], parts[...], preferred_element_type=f32)
        added = both[:, :LEV] + both[:, LEV:]
        diff_copy(g).wait()
        for q in range(GROUP):
            row = g * GROUP + q
            forced = field_ref[row] + added[q * LON : (q + 1) * LON].T
            base = base_ref[pl.ds(row, 1), :]
            top = top_ref[pl.ds(row, 1), :]
            inside = jnp.where((level >= base) & (level <= top), 1.0, 0.0)
            mean = jnp.sum(inside * forced, axis=0, keepdims=True) / (top - base + 1).astype(f32)
            convected = forced + conv_ref[pl.ds(row, 1), :] * inside * (mean - forced)
            hi, lo = split(convected)
            d_hi = diff_buf[row, 0]
            d_lo = diff_buf[row, 1]
            mixed[row] = (
                jnp.dot(d_hi, lo, preferred_element_type=f32)
                + jnp.dot(d_lo, hi, preferred_element_type=f32)
                + jnp.dot(d_hi, hi, preferred_element_type=f32)
            )
        return carry

    lax.fori_loop(0, ROWS // GROUP, group, 0)
    open_face = jnp.where(lax.axis_index("band") == BANDS - 1, 0.0, 1.0)

    def face(row):
        if row < 0:
            return before_ref[row + 2]
        if row == ROWS:
            return after_ref[0]
        return cy_ref[row] * open_face if row == ROWS - 1 else cy_ref[row]

    def partial_sweep(value, first, last, row):
        own = value(row) if first <= row <= last else None
        terms = []
        if own is not None or row - 1 >= first:
            low = jnp.minimum(face(row - 1), 0.0) if row > -2 else None
        if own is not None:
            terms.append((1.0 - jnp.maximum(face(row), 0.0) + low) * own)
        if first <= row + 1 <= last:
            terms.append(jnp.maximum(face(row), 0.0) * value(row + 1))
        if first <= row - 1 <= last:
            terms.append(-(low * value(row - 1)))
        return sum(terms[1:], terms[0])

    for row in range(-1, ROWS + 1):
        once[row + 1] = partial_sweep(lambda r: mixed[r], 0, ROWS - 1, row)
    for row in range(-2, ROWS + 2):
        value = partial_sweep(lambda r: once[r + 1], -1, ROWS, row)
        block_out[:, row + 2] = value.reshape(BANDS, SLAB, LON)


def summed(rows_ref, s, row):
    value = rows_ref[s, row + 2]
    if row < 2:
        value += jnp.where(s > 0, rows_ref[jnp.maximum(s - 1, 0), row + ROWS + 2], 0.0)
    if row >= ROWS - 2:
        value += jnp.where(s < BANDS - 1, rows_ref[jnp.minimum(s + 1, BANDS - 1), row - ROWS + 2], 0.0)
    return value


def pack_kernel(rows_ref, left_out, right_out):
    def sources(i, carry):
        for k in range(CHUNK):
            s = i * CHUNK + k
            left, right = pack_strips(lambda row: summed(rows_ref, s, row))
            for half in range(HALVES):
                left_out[s, half] = left[half]
                right_out[s, half] = right[half]
        return carry

    lax.fori_loop(0, BANDS // CHUNK, sources, 0)


def zonal_kernel(rows_ref, cx_ref, out_ref, keep_buf, up_buf, low_buf, first, second):
    tiles = CHUNK * ROWS

    def sources(i, carry):
        for t in range(tiles):
            first[t] = summed(rows_ref, i * CHUNK + t // ROWS, t % ROWS)
            keep_buf[t], up_buf[t], low_buf[t] = stencil_of(cx_ref[i * tiles + t])
        old, new = first, second
        for step in range(XSTEPS):
            for t in range(tiles):
                value = zonal_sweep(old[t], keep_buf[t], up_buf[t], low_buf[t])
                if step == XSTEPS - 1:
                    out_ref[i * tiles + t] = value
                else:
                    new[t] = value
            old, new = new, old
        return carry

    lax.fori_loop(0, BANDS // CHUNK, sources, 0)


def merge_kernel(inner_ref, left_ref, right_ref, west_ref, east_ref, coef_ref, out_ref, sides, left_buf, right_buf):
    count = BANDS * HALVES
    for n in range(count):
        s, half = n // HALVES, n % HALVES
        left_buf[n], right_buf[n] = fill_halo(
            left_ref[s, half], right_ref[s, half], west_ref[s, half], east_ref[s, half]
        )
    for _ in range(XSTEPS):
        for n in range(count):
            s, half = n // HALVES, n % HALVES
            for side, buf in enumerate((left_buf, right_buf)):
                buf[n] = zonal_sweep(buf[n], *(coef_ref[s, half, side, k] for k in range(3)))
    spot = lane_iota((SLAB, LON)) % STRIP
    for n in range(count):
        sides[n] = jnp.where(spot < XSTEPS, turned(right_buf[n], -2 * XSTEPS), left_buf[n])
    lane = lane_iota((SLAB, LON))
    outer = (lane < XSTEPS) | (lane >= LON - XSTEPS)

    def sources(i, carry):
        for k in range(HALVES):
            packed = sides[i * HALVES + k]
            for g in range(ROWS // HALVES):
                lat = i * ROWS + k * (ROWS // HALVES) + g
                out_ref[:, pl.ds(lat, 1), :] = jnp.where(
                    outer, turned(packed, -STRIP * g - XSTEPS), inner_ref[lat]
                ).reshape(SLAB, 1, LON)
        return carry

    lax.fori_loop(0, BANDS, sources, 0)


def call(body, outs, args, scratch=(), hbm_in=(), hbm_out=(), vmem=16):
    def place(k, far):
        return pl.BlockSpec(memory_space=pltpu.HBM if k in far else pltpu.VMEM)

    args = [pltpu.with_memory_space_constraint(x, pltpu.HBM) if k in hbm_in else x for k, x in enumerate(args)]
    return pl.pallas_call(
        body,
        out_shape=[
            (pltpu.HBM if k in hbm_out else jax.ShapeDtypeStruct)(shape, kind) for k, (shape, kind) in enumerate(outs)
        ],
        in_specs=[place(k, hbm_in) for k in range(len(args))],
        out_specs=[place(k, hbm_out) for k in range(len(outs))],
        scratch_shapes=list(scratch),
        compiler_params=pltpu.CompilerParams(vmem_limit_bytes=vmem << 20),
    )(*args)


def ring_pair(up_value, down_value, axis, wrap):
    n = lax.axis_size(axis)
    up = [(i, (i + 1) % n) for i in range(n if wrap else n - 1)]
    from_prev = lax.ppermute(up_value, axis, up)
    from_next = lax.ppermute(down_value, axis, [(b, a) for a, b in up])
    return from_prev, from_next


def swap_bands(blocks):
    return lax.all_to_all(blocks, "band", split_axis=0, concat_axis=0, tiled=True)


def step_adjoint(
    adjoint_in, courant_y, courant_x, diffusion_inverse, conv_weight, cloud_base, cloud_top,
    sound_count, xco2_adjoint, kernel, sound_cols,
):
    slots = kernel.shape[2]
    dma = pltpu.SemaphoreType.DMA
    (kern,) = call(
        scale_kernel,
        [(kernel.shape[1:], f32)],
        (sound_count, xco2_adjoint, kernel),
        (
            pltpu.VMEM(sound_count.shape, jnp.int32),
            pltpu.VMEM(xco2_adjoint.shape, f32),
            pltpu.VMEM(kernel.shape[1:], f32),
            dma((2,)),
            dma((BANDS // GROUP,)),
            dma((BANDS // GROUP,)),
        ),
        hbm_in=(0, 1, 2),
        hbm_out=(0,),
    )
    kern = swap_bands(kern)

    grid = (ROWS, LEV, LON)
    field, cy, diff = call(
        prepare_kernel,
        [(grid, f32), (grid, f32), ((ROWS, 2, LEV, LEV), bf16)],
        (adjoint_in, courant_y, diffusion_inverse),
        (
            pltpu.VMEM(adjoint_in.shape, f32),
            pltpu.VMEM(courant_y.shape, f32),
            pltpu.VMEM(diffusion_inverse.shape, f32),
            pltpu.VMEM((ROWS, 2, LEV, LEV), bf16),
            dma((3,)),
            dma,
        ),
        hbm_in=(0, 1, 2),
        hbm_out=(2,),
    )
    cy_before, cy_after = ring_pair(cy[ROWS - 2 :], cy[:1], "band", False)

    (rows,) = call(
        mix_kernel,
        [((BANDS, WIDE, SLAB, LON), f32)],
        (
            kern.reshape(BANDS * slots, LEV),
            sound_cols.reshape(1, BANDS * slots),
            field,
            cy,
            cy_before,
            cy_after,
            diff,
            conv_weight,
            cloud_base,
            cloud_top,
        ),
        (
            pltpu.VMEM((BANDS * slots, 2 * LEV), bf16),
            pltpu.VMEM((GROUP * LON, BANDS * slots), bf16),
            pltpu.VMEM(grid, f32),
            pltpu.VMEM((ROWS + 2, LEV, LON), f32),
            pltpu.VMEM((ROWS, 2, LEV, LEV), bf16),
            pltpu.VMEM((ROWS, LON), f32),
            pltpu.VMEM((ROWS, LON), jnp.int32),
            pltpu.VMEM((ROWS, LON), jnp.int32),
            dma((ROWS // GROUP,)),
            dma((3,)),
        ),
        hbm_in=(6, 7, 8, 9),
    )
    rows = swap_bands(rows)

    strips = (BANDS, HALVES, SLAB, LON)
    tiles = (BANDS * ROWS, SLAB, LON)
    cx, cx_left, cx_right = call(faces_kernel, [(tiles, f32), (strips, f32), (strips, f32)], (courant_x,))
    cx_west, cx_east = ring_pair(cx_right, cx_left, "region", True)
    (coef,) = call(
        sides_kernel,
        [((BANDS, HALVES, 2, 3, SLAB, LON), f32)],
        (cx_left, cx_right, cx_west, cx_east),
    )
    left, right = call(pack_kernel, [(strips, f32), (strips, f32)], (rows,))
    west, east = ring_pair(right, left, "region", True)
    chunk = pltpu.VMEM((CHUNK * ROWS, SLAB, LON), f32)
    (inner,) = call(zonal_kernel, [(tiles, f32)], (rows, cx), (chunk,) * 5)
    flat = pltpu.VMEM((BANDS * HALVES, SLAB, LON), f32)
    return call(
        merge_kernel,
        [((SLAB, BANDS * ROWS, LON), f32)],
        (inner, left, right, west, east, coef),
        (flat,) * 3,
    )[0]


def solution(mesh):
    in_specs = (
        P(None, "band", "region"),
        P(None, "band", "region"),
        P("band", None, "region"),
        P("band", None, None),
        P("band", "region"),
        P("band", "region"),
        P("band", "region"),
        P("region", "band"),
        P("region", "band", None),
        P("region", "band", None, None),
        P("region", "band", None),
    )
    out_specs = P("band", None, "region")
    return jax.shard_map(step_adjoint, mesh=mesh, in_specs=in_specs, out_specs=out_specs, check_vma=False)
```

```python
import jax
import jax.numpy as jnp
from jax import lax
from jax.experimental import pallas as pl
from jax.experimental.pallas import tpu as pltpu
from jax.sharding import PartitionSpec as P


XSTEPS = 4
LEV = 128
ROWS = 16
LON = 128
BANDS = 16
SLAB = 8
STRIP = 16
HALVES = 2
GROUP = 4
CHUNK = 4
CORES = 2
CHIPS = BANDS // CORES
ORDER = (4, 3, 5, 2, 6, 1, 7)
WIDE = ROWS + 4

f32 = jnp.float32
bf16 = jnp.bfloat16


def split(x):
    hi = x.astype(bf16)
    return hi, (x - hi.astype(f32)).astype(bf16)


def lane_iota(shape):
    return lax.broadcasted_iota(jnp.int32, shape, len(shape) - 1)


def turned(x, shift):
    shift %= LON
    return pltpu.roll(x, shift, x.ndim - 1) if shift else x


def pack_strips(tile_of):
    left, right = [], []
    for half in range(HALVES):
        west = east = None
        for g in range(ROWS // HALVES):
            tile = tile_of(half * (ROWS // HALVES) + g)
            here = lane_iota(tile.shape) // STRIP == g
            to_west = turned(tile, STRIP * g + XSTEPS)
            to_east = turned(tile, STRIP * g + STRIP - XSTEPS)
            west = to_west if west is None else jnp.where(here, to_west, west)
            east = to_east if east is None else jnp.where(here, to_east, east)
        left.append(west)
        right.append(east)
    return left, right


def scale_kernel(count_hbm, value_hbm, kern_hbm, out_hbm, count, value, kern, sem, kern_sem, out_sem):
    small = [
        pltpu.make_async_copy(count_hbm, count, sem.at[0]),
        pltpu.make_async_copy(value_hbm, value, sem.at[1]),
    ]
    spans = [pl.ds(c * GROUP, GROUP) for c in range(BANDS // GROUP)]
    loads = [pltpu.make_async_copy(kern_hbm.at[0, spans[c]], kern.at[spans[c]], kern_sem.at[c]) for c in range(len(spans))]
    stores = [pltpu.make_async_copy(kern.at[spans[c]], out_hbm.at[spans[c]], out_sem.at[c]) for c in range(len(spans))]
    for copy in small + loads:
        copy.start()
    for copy in small:
        copy.wait()
    factor = value[0].T
    live = lax.broadcasted_iota(jnp.int32, factor.shape, 0) < count[...]
    factor = jnp.where(live, factor, 0.0)
    for c in range(len(spans)):
        loads[c].wait()
        for band in range(c * GROUP, c * GROUP + GROUP):
            kern[band] = kern[band] * factor[:, band : band + 1]
        stores[c].start()
    for copy in stores:
        copy.wait()


def prepare_kernel(field_hbm, cy_hbm, diff_hbm, field_out, cy_out, diff_out, field, cy, diff, parts, sem, out_sem):
    loads = [
        pltpu.make_async_copy(diff_hbm, diff, sem.at[0]),
        pltpu.make_async_copy(field_hbm, field, sem.at[1]),
        pltpu.make_async_copy(cy_hbm, cy, sem.at[2]),
    ]
    for copy in loads:
        copy.start()
    loads[0].wait()
    for row in range(ROWS):
        hi, lo = split(diff[row].T)
        parts[row, 0] = hi
        parts[row, 1] = lo
    store = pltpu.make_async_copy(parts, diff_out, out_sem)
    store.start()
    loads[1].wait()
    for row in range(ROWS):
        field_out[row] = field[:, row, :]
    loads[2].wait()
    for row in range(ROWS):
        cy_out[row] = cy[:, row, :]
    store.wait()


def faces_kernel(cx_ref, cx_out, left_out, right_out):
    def source(s, carry):
        def tile_of(row):
            tile = cx_ref[:, pl.ds(s * ROWS + row, 1), :].reshape(SLAB, LON)
            cx_out[s * ROWS + row] = tile
            return tile

        left, right = pack_strips(tile_of)
        for half in range(HALVES):
            left_out[s, half] = left[half]
            right_out[s, half] = right[half]
        return carry

    lax.fori_loop(0, BANDS, source, 0)


def fill_halo(left, right, west, east):
    spot = lane_iota(left.shape) % STRIP
    left = jnp.where(spot < XSTEPS, turned(west, XSTEPS - STRIP + XSTEPS), left)
    right = jnp.where(spot >= STRIP - XSTEPS, turned(east, STRIP - 2 * XSTEPS), right)
    return left, right


def stencil_of(courant):
    up = jnp.maximum(courant, 0.0)
    low = turned(jnp.minimum(courant, 0.0), 1)
    return 1.0 - up + low, up, low


def zonal_sweep(value, keep, up, low):
    return keep * value + up * turned(value, -1) - low * turned(value, 1)


def sides_kernel(left_ref, right_ref, west_ref, east_ref, coef_out):
    def source(s, carry):
        for half in range(HALVES):
            strips = fill_halo(left_ref[s, half], right_ref[s, half], west_ref[s, half], east_ref[s, half])
            for side in range(2):
                for k, value in enumerate(stencil_of(strips[side])):
                    coef_out[s, half, side, k] = value
        return carry

    lax.fori_loop(0, BANDS, source, 0)


def mix_kernel(
    kern_ref, cols_ref, field_ref, cy_ref, before_ref, after_ref, diff_hbm, conv_hbm, base_hbm, top_hbm,
    keep_out, give_out,
    parts, onehot, mixed, once, twice, diff_buf, conv_ref, base_ref, top_ref, diff_sem, sem,
):
    def diff_copy(g):
        span = pl.ds(g * GROUP, GROUP)
        return pltpu.make_async_copy(diff_hbm.at[span], diff_buf.at[span], diff_sem.at[g])

    small = [
        pltpu.make_async_copy(conv_hbm, conv_ref, sem.at[0]),
        pltpu.make_async_copy(base_hbm, base_ref, sem.at[1]),
        pltpu.make_async_copy(top_hbm, top_ref, sem.at[2]),
    ]
    for copy in small + [diff_copy(g) for g in range(ROWS // GROUP)]:
        copy.start()
    for c in range(8):
        span = slice(c * 128, c * 128 + 128)
        hi, lo = split(kern_ref[span, :])
        parts[span, :LEV] = hi
        parts[span, LEV:] = lo

    for copy in small:
        copy.wait()
    level = lax.broadcasted_iota(jnp.int32, (LEV, LON), 0)

    def group(g, carry):
        cols = cols_ref[...] - g * (GROUP * LON)
        for r in range(0, GROUP * LON, 32):
            cell = lax.broadcasted_iota(jnp.int32, (32, cols.shape[1]), 0) + r
            onehot[pl.ds(r, 32), :] = jnp.where(cell == cols, 1.0, 0.0).astype(bf16)
        both = jnp.dot(onehot[...], parts[...], preferred_element_type=f32)
        added = both[:, :LEV] + both[:, LEV:]
        diff_copy(g).wait()
        for q in range(GROUP):
            row = g * GROUP + q
            forced = field_ref[row] + added[q * LON : (q + 1) * LON].T
            base = base_ref[pl.ds(row, 1), :]
            top = top_ref[pl.ds(row, 1), :]
            inside = jnp.where((level >= base) & (level <= top), 1.0, 0.0)
            mean = jnp.sum(inside * forced, axis=0, keepdims=True) / (top - base + 1).astype(f32)
            convected = forced + conv_ref[pl.ds(row, 1), :] * inside * (mean - forced)
            hi, lo = split(convected)
            d_hi = diff_buf[row, 0]
            d_lo = diff_buf[row, 1]
            mixed[row] = (
                jnp.dot(d_hi, lo, preferred_element_type=f32)
                + jnp.dot(d_lo, hi, preferred_element_type=f32)
                + jnp.dot(d_hi, hi, preferred_element_type=f32)
            )
        return carry

    lax.fori_loop(0, ROWS // GROUP, group, 0)
    open_face = jnp.where(lax.axis_index("band") == BANDS - 1, 0.0, 1.0)

    def face(row):
        if row < 0:
            return before_ref[row + 2]
        if row == ROWS:
            return after_ref[0]
        return cy_ref[row] * open_face if row == ROWS - 1 else cy_ref[row]

    def partial_sweep(value, first, last, row):
        own = value(row) if first <= row <= last else None
        terms = []
        if own is not None or row - 1 >= first:
            low = jnp.minimum(face(row - 1), 0.0) if row > -2 else None
        if own is not None:
            terms.append((1.0 - jnp.maximum(face(row), 0.0) + low) * own)
        if first <= row + 1 <= last:
            terms.append(jnp.maximum(face(row), 0.0) * value(row + 1))
        if first <= row - 1 <= last:
            terms.append(-(low * value(row - 1)))
        return sum(terms[1:], terms[0])

    for row in range(-1, ROWS + 1):
        once[row + 1] = partial_sweep(lambda r: mixed[r], 0, ROWS - 1, row)
    for row in range(-2, ROWS + 2):
        value = partial_sweep(lambda r: once[r + 1], -1, ROWS, row)
        twice[row + 2] = value
    z, core = lax.axis_index("band") // CORES, lax.axis_index("band") % CORES
    for t in range(CHIPS):
        pair = CORES * ((z + t) % CHIPS)
        for row in range(WIDE):
            keep_out[t, row] = twice[row, pl.ds(pl.multiple_of((pair + core) * SLAB, SLAB), SLAB)]
            give_out[t, row] = twice[row, pl.ds(pl.multiple_of((pair + 1 - core) * SLAB, SLAB), SLAB)]


def join_kernel(keep_ref, got_ref, *outs):
    core = lax.axis_index("band") % CORES
    for t in range(CHIPS):
        outs[t][core] = keep_ref[t]
        outs[t][1 - core] = got_ref[t]


def pack_kernel(*refs):
    moved, (own_out, left_out, right_out) = refs[:CHIPS], refs[CHIPS:]
    z = lax.axis_index("band") // CORES
    sources = [
        (moved[t], core, CORES * ((z - t) % CHIPS) + core) for t in range(CHIPS) for core in range(CORES)
    ]
    for ref, core, s in sources:
        own_out[pl.ds(s * ROWS, ROWS)] = ref[core, 2 : ROWS + 2]
    for ref, core, s in sources:
        south = pl.ds(jnp.maximum(s - 1, 0) * ROWS + ROWS - 2, 2)
        own_out[south] += jnp.where(s > 0, ref[core, 0:2], 0.0)
        north = pl.ds(jnp.minimum(s + 1, BANDS - 1) * ROWS, 2)
        own_out[north] += jnp.where(s < BANDS - 1, ref[core, ROWS + 2 :], 0.0)

    def pack(i, carry):
        for k in range(CHUNK):
            s = i * CHUNK + k
            left, right = pack_strips(lambda row: own_out[s * ROWS + row])
            for half in range(HALVES):
                left_out[s, half] = left[half]
                right_out[s, half] = right[half]
        return carry

    lax.fori_loop(0, BANDS // CHUNK, pack, 0)


def zonal_kernel(own_ref, cx_ref, out_ref, keep_buf, up_buf, low_buf, first, second):
    tiles = CHUNK * ROWS

    def sources(i, carry):
        for t in range(tiles):
            keep_buf[t], up_buf[t], low_buf[t] = stencil_of(cx_ref[i * tiles + t])
        old, new = first, second
        for step in range(XSTEPS):
            for t in range(tiles):
                value = own_ref[i * tiles + t] if step == 0 else old[t]
                value = zonal_sweep(value, keep_buf[t], up_buf[t], low_buf[t])
                if step == XSTEPS - 1:
                    out_ref[i * tiles + t] = value
                else:
                    new[t] = value
            old, new = new, old
        return carry

    lax.fori_loop(0, BANDS // CHUNK, sources, 0)


def merge_kernel(inner_ref, left_ref, right_ref, west_ref, east_ref, coef_ref, out_ref, sides, left_buf, right_buf):
    count = BANDS * HALVES
    for n in range(count):
        s, half = n // HALVES, n % HALVES
        left_buf[n], right_buf[n] = fill_halo(
            left_ref[s, half], right_ref[s, half], west_ref[s, half], east_ref[s, half]
        )
    for _ in range(XSTEPS):
        for n in range(count):
            s, half = n // HALVES, n % HALVES
            for side, buf in enumerate((left_buf, right_buf)):
                buf[n] = zonal_sweep(buf[n], *(coef_ref[s, half, side, k] for k in range(3)))
    spot = lane_iota((SLAB, LON)) % STRIP
    for n in range(count):
        sides[n] = jnp.where(spot < XSTEPS, turned(right_buf[n], -2 * XSTEPS), left_buf[n])
    lane = lane_iota((SLAB, LON))
    outer = (lane < XSTEPS) | (lane >= LON - XSTEPS)

    def sources(i, carry):
        for k in range(HALVES):
            packed = sides[i * HALVES + k]
            for g in range(ROWS // HALVES):
                lat = i * ROWS + k * (ROWS // HALVES) + g
                out_ref[:, pl.ds(lat, 1), :] = jnp.where(
                    outer, turned(packed, -STRIP * g - XSTEPS), inner_ref[lat]
                ).reshape(SLAB, 1, LON)
        return carry

    lax.fori_loop(0, BANDS, sources, 0)


def call(body, outs, args, scratch=(), hbm_in=(), hbm_out=(), vmem=16):
    def place(k, far):
        return pl.BlockSpec(memory_space=pltpu.HBM if k in far else pltpu.VMEM)

    args = [pltpu.with_memory_space_constraint(x, pltpu.HBM) if k in hbm_in else x for k, x in enumerate(args)]
    return pl.pallas_call(
        body,
        out_shape=[
            (pltpu.HBM if k in hbm_out else jax.ShapeDtypeStruct)(shape, kind) for k, (shape, kind) in enumerate(outs)
        ],
        in_specs=[place(k, hbm_in) for k in range(len(args))],
        out_specs=[place(k, hbm_out) for k in range(len(outs))],
        scratch_shapes=list(scratch),
        compiler_params=pltpu.CompilerParams(vmem_limit_bytes=vmem << 20),
    )(*args)


def ring_pair(up_value, down_value, axis, wrap):
    n = lax.axis_size(axis)
    up = [(i, (i + 1) % n) for i in range(n if wrap else n - 1)]
    from_prev = lax.ppermute(up_value, axis, up)
    from_next = lax.ppermute(down_value, axis, [(b, a) for a, b in up])
    return from_prev, from_next


def swap_bands(blocks):
    return lax.all_to_all(blocks, "band", split_axis=0, concat_axis=0, tiled=True)


def step_adjoint(
    adjoint_in, courant_y, courant_x, diffusion_inverse, conv_weight, cloud_base, cloud_top,
    sound_count, xco2_adjoint, kernel, sound_cols,
):
    slots = kernel.shape[2]
    dma = pltpu.SemaphoreType.DMA
    (kern,) = call(
        scale_kernel,
        [(kernel.shape[1:], f32)],
        (sound_count, xco2_adjoint, kernel),
        (
            pltpu.VMEM(sound_count.shape, jnp.int32),
            pltpu.VMEM(xco2_adjoint.shape, f32),
            pltpu.VMEM(kernel.shape[1:], f32),
            dma((2,)),
            dma((BANDS // GROUP,)),
            dma((BANDS // GROUP,)),
        ),
        hbm_in=(0, 1, 2),
        hbm_out=(0,),
    )
    kern = swap_bands(kern)

    grid = (ROWS, LEV, LON)
    field, cy, diff = call(
        prepare_kernel,
        [(grid, f32), (grid, f32), ((ROWS, 2, LEV, LEV), bf16)],
        (adjoint_in, courant_y, diffusion_inverse),
        (
            pltpu.VMEM(adjoint_in.shape, f32),
            pltpu.VMEM(courant_y.shape, f32),
            pltpu.VMEM(diffusion_inverse.shape, f32),
            pltpu.VMEM((ROWS, 2, LEV, LEV), bf16),
            dma((3,)),
            dma,
        ),
        hbm_in=(0, 1, 2),
        hbm_out=(2,),
    )
    cy_before, cy_after = ring_pair(cy[ROWS - 2 :], cy[:1], "band", False)

    keep, give = call(
        mix_kernel,
        [((CHIPS, WIDE, SLAB, LON), f32)] * 2,
        (
            kern.reshape(BANDS * slots, LEV),
            sound_cols.reshape(1, BANDS * slots),
            field,
            cy,
            cy_before,
            cy_after,
            diff,
            conv_weight,
            cloud_base,
            cloud_top,
        ),
        (
            pltpu.VMEM((BANDS * slots, 2 * LEV), bf16),
            pltpu.VMEM((GROUP * LON, BANDS * slots), bf16),
            pltpu.VMEM(grid, f32),
            pltpu.VMEM((ROWS + 2, LEV, LON), f32),
            pltpu.VMEM((WIDE, LEV, LON), f32),
            pltpu.VMEM((ROWS, 2, LEV, LEV), bf16),
            pltpu.VMEM((ROWS, LON), f32),
            pltpu.VMEM((ROWS, LON), jnp.int32),
            pltpu.VMEM((ROWS, LON), jnp.int32),
            dma((ROWS // GROUP,)),
            dma((3,)),
        ),
        hbm_in=(6, 7, 8, 9),
    )
    got = lax.ppermute(give, "band", [(i, i ^ 1) for i in range(BANDS)])
    moved = list(call(join_kernel, [((CORES, WIDE, SLAB, LON), f32)] * CHIPS, (keep, got)))
    for t in ORDER:
        moved[t] = lax.ppermute(moved[t], "band", [(i, (i + CORES * t) % BANDS) for i in range(BANDS)])

    strips = (BANDS, HALVES, SLAB, LON)
    tiles = (BANDS * ROWS, SLAB, LON)
    cx, cx_left, cx_right = call(faces_kernel, [(tiles, f32), (strips, f32), (strips, f32)], (courant_x,))
    cx_west, cx_east = ring_pair(cx_right, cx_left, "region", True)
    (coef,) = call(
        sides_kernel,
        [((BANDS, HALVES, 2, 3, SLAB, LON), f32)],
        (cx_left, cx_right, cx_west, cx_east),
    )
    own, left, right = call(pack_kernel, [(tiles, f32), (strips, f32), (strips, f32)], tuple(moved))
    west, east = ring_pair(right, left, "region", True)
    chunk = pltpu.VMEM((CHUNK * ROWS, SLAB, LON), f32)
    (inner,) = call(zonal_kernel, [(tiles, f32)], (own, cx), (chunk,) * 5)
    flat = pltpu.VMEM((BANDS * HALVES, SLAB, LON), f32)
    return call(
        merge_kernel,
        [((SLAB, BANDS * ROWS, LON), f32)],
        (inner, left, right, west, east, coef),
        (flat,) * 3,
    )[0]


def solution(mesh):
    in_specs = (
        P(None, "band", "region"),
        P(None, "band", "region"),
        P("band", None, "region"),
        P("band", None, None),
        P("band", "region"),
        P("band", "region"),
        P("band", "region"),
        P("region", "band"),
        P("region", "band", None),
        P("region", "band", None, None),
        P("region", "band", None),
    )
    out_specs = P("band", None, "region")
    return jax.shard_map(step_adjoint, mesh=mesh, in_specs=in_specs, out_specs=out_specs, check_vma=False)
```

```python
import jax
import jax.numpy as jnp
from jax import lax
from jax.experimental import pallas as pl
from jax.experimental.pallas import tpu as pltpu
from jax.sharding import PartitionSpec as P


XSTEPS = 4
LEV = 128
ROWS = 16
LON = 128
BANDS = 16
SLAB = 8
STRIP = 16
HALVES = 2
GROUP = 4
CHUNK = 4
CORES = 2
CHIPS = BANDS // CORES
FAR = CHIPS // 2
NEAR = (0, 3, 5, 2, 6, 1, 7)
WIDE = ROWS + 4

f32 = jnp.float32
bf16 = jnp.bfloat16


def split(x):
    hi = x.astype(bf16)
    return hi, (x - hi.astype(f32)).astype(bf16)


def lane_iota(shape):
    return lax.broadcasted_iota(jnp.int32, shape, len(shape) - 1)


def turned(x, shift):
    shift %= LON
    return pltpu.roll(x, shift, x.ndim - 1) if shift else x


def pack_strips(tile_of):
    left, right = [], []
    for half in range(HALVES):
        west = east = None
        for g in range(ROWS // HALVES):
            tile = tile_of(half * (ROWS // HALVES) + g)
            here = lane_iota(tile.shape) // STRIP == g
            to_west = turned(tile, STRIP * g + XSTEPS)
            to_east = turned(tile, STRIP * g + STRIP - XSTEPS)
            west = to_west if west is None else jnp.where(here, to_west, west)
            east = to_east if east is None else jnp.where(here, to_east, east)
        left.append(west)
        right.append(east)
    return left, right


def scale_kernel(count_hbm, value_hbm, kern_hbm, out_ref, count, value, kern, sem, kern_sem):
    small = [
        pltpu.make_async_copy(count_hbm, count, sem.at[0]),
        pltpu.make_async_copy(value_hbm, value, sem.at[1]),
    ]
    spans = [pl.ds(c * GROUP, GROUP) for c in range(BANDS // GROUP)]
    loads = [pltpu.make_async_copy(kern_hbm.at[0, spans[c]], kern.at[spans[c]], kern_sem.at[c]) for c in range(len(spans))]
    for copy in small + loads:
        copy.start()
    for copy in small:
        copy.wait()
    factor = value[0].T
    live = lax.broadcasted_iota(jnp.int32, factor.shape, 0) < count[...]
    factor = jnp.where(live, factor, 0.0)
    for c in range(len(spans)):
        loads[c].wait()
        for band in range(c * GROUP, c * GROUP + GROUP):
            out_ref[band] = kern[band] * factor[:, band : band + 1]


def prepare_kernel(field_hbm, cy_hbm, diff_hbm, field_out, cy_out, diff_out, field, cy, diff, parts, sem, out_sem):
    loads = [
        pltpu.make_async_copy(diff_hbm, diff, sem.at[0]),
        pltpu.make_async_copy(field_hbm, field, sem.at[1]),
        pltpu.make_async_copy(cy_hbm, cy, sem.at[2]),
    ]
    for copy in loads:
        copy.start()
    loads[0].wait()
    for row in range(ROWS):
        hi, lo = split(diff[row].T)
        parts[row, :, :LEV] = hi
        parts[row, :, LEV:] = lo
    store = pltpu.make_async_copy(parts, diff_out, out_sem)
    store.start()
    loads[1].wait()
    for row in range(ROWS):
        field_out[row] = field[:, row, :]
    loads[2].wait()
    for row in range(ROWS):
        cy_out[row] = cy[:, row, :]
    store.wait()


def faces_kernel(cx_ref, cx_out, low_out, left_out, right_out):
    def sources(i, carry):
        for k in range(2):
            s = i * 2 + k

            def tile_of(row):
                tile = cx_ref[:, pl.ds(s * ROWS + row, 1), :].reshape(SLAB, LON)
                cx_out[s * ROWS + row] = tile
                low_out[s * ROWS + row] = turned(jnp.minimum(tile, 0.0), 1)
                return tile

            left, right = pack_strips(tile_of)
            for half in range(HALVES):
                left_out[s, half] = left[half]
                right_out[s, half] = right[half]
        return carry

    lax.fori_loop(0, BANDS // 2, sources, 0)


def fill_halo(left, right, west, east):
    spot = lane_iota(left.shape) % STRIP
    left = jnp.where(spot < XSTEPS, turned(west, XSTEPS - STRIP + XSTEPS), left)
    right = jnp.where(spot >= STRIP - XSTEPS, turned(east, STRIP - 2 * XSTEPS), right)
    return left, right


def stencil_of(courant):
    up = jnp.maximum(courant, 0.0)
    low = turned(jnp.minimum(courant, 0.0), 1)
    return 1.0 - up + low, up, low


def zonal_sweep(value, keep, up, low):
    return keep * value + up * turned(value, -1) - low * turned(value, 1)


def sides_kernel(left_ref, right_ref, west_ref, east_ref, coef_out):
    def sources(i, carry):
        for k in range(CHUNK):
            s = i * CHUNK + k
            for half in range(HALVES):
                strips = fill_halo(left_ref[s, half], right_ref[s, half], west_ref[s, half], east_ref[s, half])
                for side in range(2):
                    for n, value in enumerate(stencil_of(strips[side])):
                        coef_out[s, half, side, n] = value
        return carry

    lax.fori_loop(0, BANDS // CHUNK, sources, 0)


def mix_kernel(
    kern_ref, cols_ref, field_ref, cy_ref, before_ref, after_ref, diff_hbm, conv_hbm, base_hbm, top_hbm,
    keep_out, give_out, far_out,
    parts, onehot, mixed, once, twice, diff_buf, conv_ref, base_ref, top_ref, diff_sem, sem,
):
    def diff_copy(g):
        span = pl.ds(g * GROUP, GROUP)
        return pltpu.make_async_copy(diff_hbm.at[span], diff_buf.at[span], diff_sem.at[g])

    small = [
        pltpu.make_async_copy(conv_hbm, conv_ref, sem.at[0]),
        pltpu.make_async_copy(base_hbm, base_ref, sem.at[1]),
        pltpu.make_async_copy(top_hbm, top_ref, sem.at[2]),
    ]
    for copy in small + [diff_copy(g) for g in range(ROWS // GROUP)]:
        copy.start()
    for c in range(8):
        span = slice(c * 128, c * 128 + 128)
        hi, lo = split(kern_ref[span, :])
        parts[span, :LEV] = hi
        parts[span, LEV:] = lo

    for copy in small:
        copy.wait()
    level = lax.broadcasted_iota(jnp.int32, (LEV, LON), 0)

    for g in range(ROWS // GROUP):
        cols = cols_ref[...]
        for q in range(GROUP):
            here = jnp.where(cols // LON == g * GROUP + q, cols % LON, -1).astype(f32).astype(bf16)
            for r in range(0, LON, 32):
                cell = lax.broadcasted_iota(jnp.int32, (32, cols.shape[1]), 0) + r
                match = cell.astype(f32).astype(bf16) == here
                onehot[g, q * LON + r : q * LON + r + 32, :] = jnp.where(match, jnp.ones((), bf16), jnp.zeros((), bf16))
        both = jnp.dot(onehot[g], parts[...], preferred_element_type=f32)
        added = both[:, :LEV] + both[:, LEV:]
        diff_copy(g).wait()
        for q in range(GROUP):
            row = g * GROUP + q
            forced = field_ref[row] + added[q * LON : (q + 1) * LON].T
            base = base_ref[row : row + 1, :]
            top = top_ref[row : row + 1, :]
            inside = jnp.where((level >= base) & (level <= top), 1.0, 0.0)
            mean = jnp.sum(inside * forced, axis=0, keepdims=True) / (top - base + 1).astype(f32)
            convected = forced + conv_ref[row : row + 1, :] * inside * (mean - forced)
            hi, lo = split(convected)
            pair = jnp.concatenate([hi, lo], axis=1)
            both = jnp.dot(diff_buf[row], jnp.concatenate([pair, pair], axis=0), preferred_element_type=f32)
            mixed[row] = both[:, :LON] + both[:, LON:]
    open_face = jnp.where(lax.axis_index("band") == BANDS - 1, 0.0, 1.0)

    def face(row):
        if row < 0:
            return before_ref[row + 2]
        if row == ROWS:
            return after_ref[0]
        return cy_ref[row] * open_face if row == ROWS - 1 else cy_ref[row]

    def partial_sweep(value, first, last, row):
        own = value(row) if first <= row <= last else None
        terms = []
        if own is not None or row - 1 >= first:
            low = jnp.minimum(face(row - 1), 0.0) if row > -2 else None
        if own is not None:
            terms.append((1.0 - jnp.maximum(face(row), 0.0) + low) * own)
        if first <= row + 1 <= last:
            terms.append(jnp.maximum(face(row), 0.0) * value(row + 1))
        if first <= row - 1 <= last:
            terms.append(-(low * value(row - 1)))
        return sum(terms[1:], terms[0])

    for row in range(-1, ROWS + 1):
        once[row + 1] = partial_sweep(lambda r: mixed[r], 0, ROWS - 1, row)
    for row in range(-2, ROWS + 2):
        value = partial_sweep(lambda r: once[r + 1], -1, ROWS, row)
        twice[row + 2] = value
    z, core = lax.axis_index("band") // CORES, lax.axis_index("band") % CORES
    for t in range(CHIPS):
        pair = CORES * ((z + t) % CHIPS)
        for row in range(WIDE):
            keep_out[t, row] = twice[row, pl.ds(pl.multiple_of((pair + core) * SLAB, SLAB), SLAB)]
            give_out[t, row] = twice[row, pl.ds(pl.multiple_of((pair + 1 - core) * SLAB, SLAB), SLAB)]
    far_out[...] = keep_out[FAR]


def join_kernel(keep_ref, got_ref, *outs):
    core = lax.axis_index("band") % CORES

    def join(south, north):
        for out, t in zip(outs[1:], NEAR):
            out[0 : ROWS + 2] = south[t, 0 : ROWS + 2]
            out[ROWS + 2 :] = north[t, 2:]
            out[ROWS : ROWS + 2] += north[t, 0:2]
            out[ROWS + 2 : ROWS + 4] += south[t, ROWS + 2 :]

    outs[0][...] = got_ref[FAR]
    pl.when(core == 0)(lambda: join(keep_ref, got_ref))
    pl.when(core == 1)(lambda: join(got_ref, keep_ref))


def pack_kernel(*refs):
    moved, (own_out, left_out, right_out) = refs[: CHIPS + 1], refs[CHIPS + 1 :]
    z, core = lax.axis_index("band") // CORES, lax.axis_index("band") % CORES
    far = (z - FAR) % CHIPS * CORES
    blocks = [(moved[0], far + core, 1), (moved[1], far + 1 - core, 1)]
    blocks += [(ref, (z - t) % CHIPS * CORES, CORES) for ref, t in zip(moved[2:], NEAR)]
    for ref, s, n in blocks:
        own_out[pl.ds(s * ROWS, n * ROWS)] = ref[2 : n * ROWS + 2]
    for ref, s, n in blocks:
        south = pl.ds(jnp.maximum(s - 1, 0) * ROWS + ROWS - 2, 2)
        own_out[south] += jnp.where(s > 0, ref[0:2], 0.0)
        north = pl.ds(jnp.minimum(s + n, BANDS - 1) * ROWS, 2)
        own_out[north] += jnp.where(s + n < BANDS, ref[n * ROWS + 2 :], 0.0)

    def pack(i, carry):
        for k in range(CHUNK):
            s = i * CHUNK + k
            left, right = pack_strips(lambda row: own_out[s * ROWS + row])
            for half in range(HALVES):
                left_out[s, half] = left[half]
                right_out[s, half] = right[half]
        return carry

    lax.fori_loop(0, BANDS // CHUNK, pack, 0)


def zonal_kernel(own_ref, cx_ref, low_ref, out_ref, first, second):
    tiles = CHUNK * ROWS

    def sources(i, carry):
        old, new = first, second
        for step in range(XSTEPS):
            for t in range(tiles):
                value = own_ref[i * tiles + t] if step == 0 else old[t]
                up = jnp.maximum(cx_ref[i * tiles + t], 0.0)
                low = low_ref[i * tiles + t]
                value = zonal_sweep(value, 1.0 - up + low, up, low)
                if step == XSTEPS - 1:
                    out_ref[i * tiles + t] = value
                else:
                    new[t] = value
            old, new = new, old
        return carry

    lax.fori_loop(0, BANDS // CHUNK, sources, 0)


def merge_kernel(inner_ref, left_ref, right_ref, west_ref, east_ref, coef_ref, out_hbm, sides, left_buf, right_buf, out_ref, sem):
    count = BANDS * HALVES
    for n in range(count):
        s, half = n // HALVES, n % HALVES
        left_buf[n], right_buf[n] = fill_halo(
            left_ref[s, half], right_ref[s, half], west_ref[s, half], east_ref[s, half]
        )
    for _ in range(XSTEPS):
        for n in range(count):
            s, half = n // HALVES, n % HALVES
            for side, buf in enumerate((left_buf, right_buf)):
                buf[n] = zonal_sweep(buf[n], *(coef_ref[s, half, side, k] for k in range(3)))
    spot = lane_iota((SLAB, LON)) % STRIP
    for n in range(count):
        sides[n] = jnp.where(spot < XSTEPS, turned(right_buf[n], -2 * XSTEPS), left_buf[n])
    lane = lane_iota((SLAB, LON))
    outer = (lane < XSTEPS) | (lane >= LON - XSTEPS)

    def store(c):
        span = pl.ds(c * CHUNK * ROWS, CHUNK * ROWS)
        return pltpu.make_async_copy(out_ref.at[:, span], out_hbm.at[:, span], sem.at[c])

    for c in range(BANDS // CHUNK):
        for i in range(c * CHUNK, c * CHUNK + CHUNK):
            for k in range(HALVES):
                packed = sides[i * HALVES + k]
                for g in range(ROWS // HALVES):
                    lat = i * ROWS + k * (ROWS // HALVES) + g
                    out_ref[:, lat, :] = jnp.where(outer, turned(packed, -STRIP * g - XSTEPS), inner_ref[lat])
        store(c).start()
    for c in range(BANDS // CHUNK):
        store(c).wait()


def call(body, outs, args, scratch=(), hbm_in=(), hbm_out=(), vmem=16):
    def place(k, far):
        return pl.BlockSpec(memory_space=pltpu.HBM if k in far else pltpu.VMEM)

    args = [pltpu.with_memory_space_constraint(x, pltpu.HBM) if k in hbm_in else x for k, x in enumerate(args)]
    return pl.pallas_call(
        body,
        out_shape=[
            (pltpu.HBM if k in hbm_out else jax.ShapeDtypeStruct)(shape, kind) for k, (shape, kind) in enumerate(outs)
        ],
        in_specs=[place(k, hbm_in) for k in range(len(args))],
        out_specs=[place(k, hbm_out) for k in range(len(outs))],
        scratch_shapes=list(scratch),
        compiler_params=pltpu.CompilerParams(vmem_limit_bytes=vmem << 20),
    )(*args)


def ring_pair(up_value, down_value, axis, wrap):
    n = lax.axis_size(axis)
    up = [(i, (i + 1) % n) for i in range(n if wrap else n - 1)]
    from_prev = lax.ppermute(up_value, axis, up)
    from_next = lax.ppermute(down_value, axis, [(b, a) for a, b in up])
    return from_prev, from_next


def swap_bands(blocks):
    return lax.all_to_all(blocks, "band", split_axis=0, concat_axis=0, tiled=True)


def step_adjoint(
    adjoint_in, courant_y, courant_x, diffusion_inverse, conv_weight, cloud_base, cloud_top,
    sound_count, xco2_adjoint, kernel, sound_cols,
):
    slots = kernel.shape[2]
    dma = pltpu.SemaphoreType.DMA
    (kern,) = call(
        scale_kernel,
        [(kernel.shape[1:], f32)],
        (sound_count, xco2_adjoint, kernel),
        (
            pltpu.VMEM(sound_count.shape, jnp.int32),
            pltpu.VMEM(xco2_adjoint.shape, f32),
            pltpu.VMEM(kernel.shape[1:], f32),
            dma((2,)),
            dma((BANDS // GROUP,)),
        ),
        hbm_in=(0, 1, 2),
    )
    kern = swap_bands(kern)

    grid = (ROWS, LEV, LON)
    field, cy, diff = call(
        prepare_kernel,
        [(grid, f32), (grid, f32), ((ROWS, LEV, 2 * LEV), bf16)],
        (adjoint_in, courant_y, diffusion_inverse),
        (
            pltpu.VMEM(adjoint_in.shape, f32),
            pltpu.VMEM(courant_y.shape, f32),
            pltpu.VMEM(diffusion_inverse.shape, f32),
            pltpu.VMEM((ROWS, LEV, 2 * LEV), bf16),
            dma((3,)),
            dma,
        ),
        hbm_in=(0, 1, 2),
        hbm_out=(2,),
    )
    cy_before, cy_after = ring_pair(cy[ROWS - 2 :], cy[:1], "band", False)

    keep, give, far = call(
        mix_kernel,
        [((CHIPS, WIDE, SLAB, LON), f32)] * 2 + [((WIDE, SLAB, LON), f32)],
        (
            kern.reshape(BANDS * slots, LEV),
            sound_cols.reshape(1, BANDS * slots),
            field,
            cy,
            cy_before,
            cy_after,
            diff,
            conv_weight,
            cloud_base,
            cloud_top,
        ),
        (
            pltpu.VMEM((BANDS * slots, 2 * LEV), bf16),
            pltpu.VMEM((ROWS // GROUP, GROUP * LON, BANDS * slots), bf16),
            pltpu.VMEM(grid, f32),
            pltpu.VMEM((ROWS + 2, LEV, LON), f32),
            pltpu.VMEM((WIDE, LEV, LON), f32),
            pltpu.VMEM((ROWS, LEV, 2 * LEV), bf16),
            pltpu.VMEM((ROWS, LON), f32),
            pltpu.VMEM((ROWS, LON), jnp.int32),
            pltpu.VMEM((ROWS, LON), jnp.int32),
            dma((ROWS // GROUP,)),
            dma((3,)),
        ),
        hbm_in=(6, 7, 8, 9),
        vmem=24,
    )
    got = lax.ppermute(give, "band", [(i, i ^ 1) for i in range(BANDS)])

    def move(block, t):
        return lax.ppermute(block, "band", [(i, (i + CORES * t) % BANDS) for i in range(BANDS)])

    far = move(far, FAR)
    rest, *near = call(
        join_kernel,
        [((WIDE, SLAB, LON), f32)] + [((ROWS + WIDE, SLAB, LON), f32)] * len(NEAR),
        (keep, got),
    )
    near = [near[0]] + [move(block, t) for block, t in zip(near[1:], NEAR[1:])]
    moved = (far, move(rest, FAR), *near)

    strips = (BANDS, HALVES, SLAB, LON)
    tiles = (BANDS * ROWS, SLAB, LON)
    cx, cx_low, cx_left, cx_right = call(faces_kernel, [(tiles, f32), (tiles, f32), (strips, f32), (strips, f32)], (courant_x,))
    cx_west, cx_east = ring_pair(cx_right, cx_left, "region", True)
    (coef,) = call(
        sides_kernel,
        [((BANDS, HALVES, 2, 3, SLAB, LON), f32)],
        (cx_left, cx_right, cx_west, cx_east),
    )
    own, left, right = call(pack_kernel, [(tiles, f32), (strips, f32), (strips, f32)], moved)
    west, east = ring_pair(right, left, "region", True)
    chunk = pltpu.VMEM((CHUNK * ROWS, SLAB, LON), f32)
    (inner,) = call(zonal_kernel, [(tiles, f32)], (own, cx, cx_low), (chunk,) * 2)
    flat = pltpu.VMEM((BANDS * HALVES, SLAB, LON), f32)
    return call(
        merge_kernel,
        [((SLAB, BANDS * ROWS, LON), f32)],
        (inner, left, right, west, east, coef),
        (flat,) * 3 + (pltpu.VMEM((SLAB, BANDS * ROWS, LON), f32), dma((BANDS // CHUNK,))),
        hbm_out=(0,),
    )[0]


def solution(mesh):
    in_specs = (
        P(None, "band", "region"),
        P(None, "band", "region"),
        P("band", None, "region"),
        P("band", None, None),
        P("band", "region"),
        P("band", "region"),
        P("band", "region"),
        P("region", "band"),
        P("region", "band", None),
        P("region", "band", None, None),
        P("region", "band", None),
    )
    out_specs = P("band", None, "region")
    return jax.shard_map(step_adjoint, mesh=mesh, in_specs=in_specs, out_specs=out_specs, check_vma=False)
```

```python
import functools

import jax
import jax.numpy as jnp
from jax import lax
from jax.experimental import pallas as pl
from jax.experimental.pallas import tpu as pltpu
from jax.sharding import PartitionSpec as P


XSTEPS = 4
LEV = 128
ROWS = 16
LON = 128
BANDS = 16
SLAB = 8
STRIP = 16
HALVES = 2
GROUP = 4
CHUNK = 4
CORES = 2
CHIPS = BANDS // CORES
FAR = CHIPS // 2
NEAR = (0, 3, 5, 2, 6, 1, 7)
WIDE = ROWS + 4

f32 = jnp.float32
bf16 = jnp.bfloat16


def split(x):
    hi = x.astype(bf16)
    return hi, (x - hi.astype(f32)).astype(bf16)


def lane_iota(shape):
    return lax.broadcasted_iota(jnp.int32, shape, len(shape) - 1)


def turned(x, shift):
    shift %= LON
    return pltpu.roll(x, shift, x.ndim - 1) if shift else x


def pack_strips(tile_of):
    left, right = [], []
    for half in range(HALVES):
        west = east = None
        for g in range(ROWS // HALVES):
            tile = tile_of(half * (ROWS // HALVES) + g)
            here = lane_iota(tile.shape) // STRIP == g
            to_west = turned(tile, STRIP * g + XSTEPS)
            to_east = turned(tile, STRIP * g + STRIP - XSTEPS)
            west = to_west if west is None else jnp.where(here, to_west, west)
            east = to_east if east is None else jnp.where(here, to_east, east)
        left.append(west)
        right.append(east)
    return left, right


def scale_kernel(count_hbm, value_hbm, kern_hbm, out_ref, count, value, kern, sem, kern_sem):
    small = [
        pltpu.make_async_copy(count_hbm, count, sem.at[0]),
        pltpu.make_async_copy(value_hbm, value, sem.at[1]),
    ]
    spans = [pl.ds(c * GROUP, GROUP) for c in range(BANDS // GROUP)]
    loads = [pltpu.make_async_copy(kern_hbm.at[0, spans[c]], kern.at[spans[c]], kern_sem.at[c]) for c in range(len(spans))]
    for copy in small + loads:
        copy.start()
    for copy in small:
        copy.wait()
    factor = value[0].T
    live = lax.broadcasted_iota(jnp.int32, factor.shape, 0) < count[...]
    factor = jnp.where(live, factor, 0.0)
    for c in range(len(spans)):
        loads[c].wait()
        for band in range(c * GROUP, c * GROUP + GROUP):
            out_ref[band] = kern[band] * factor[:, band : band + 1]


def prepare_kernel(field_hbm, cy_hbm, diff_hbm, field_out, cy_out, diff_out, field, cy, diff, parts, sem, out_sem):
    loads = [
        pltpu.make_async_copy(diff_hbm, diff, sem.at[0]),
        pltpu.make_async_copy(field_hbm, field, sem.at[1]),
        pltpu.make_async_copy(cy_hbm, cy, sem.at[2]),
    ]
    for copy in loads:
        copy.start()
    loads[0].wait()
    for row in range(ROWS):
        hi, lo = split(diff[row].T)
        parts[row, :, :LEV] = hi
        parts[row, :, LEV:] = lo
    store = pltpu.make_async_copy(parts, diff_out, out_sem)
    store.start()
    loads[1].wait()
    for row in range(ROWS):
        field_out[row] = field[:, row, :]
    loads[2].wait()
    for row in range(ROWS):
        cy_out[row] = cy[:, row, :]
    store.wait()


def faces_kernel(cx_ref, cx_out, low_out, left_out, right_out):
    def sources(i, carry):
        for k in range(2):
            s = i * 2 + k

            def tile_of(row):
                tile = cx_ref[:, pl.ds(s * ROWS + row, 1), :].reshape(SLAB, LON)
                cx_out[s * ROWS + row] = tile
                low_out[s * ROWS + row] = turned(jnp.minimum(tile, 0.0), 1)
                return tile

            left, right = pack_strips(tile_of)
            for half in range(HALVES):
                left_out[s, half] = left[half]
                right_out[s, half] = right[half]
        return carry

    lax.fori_loop(0, BANDS // 2, sources, 0)


def fill_halo(left, right, west, east):
    spot = lane_iota(left.shape) % STRIP
    left = jnp.where(spot < XSTEPS, turned(west, XSTEPS - STRIP + XSTEPS), left)
    right = jnp.where(spot >= STRIP - XSTEPS, turned(east, STRIP - 2 * XSTEPS), right)
    return left, right


def stencil_of(courant):
    up = jnp.maximum(courant, 0.0)
    low = turned(jnp.minimum(courant, 0.0), 1)
    return 1.0 - up + low, up, low


def zonal_sweep(value, keep, up, low):
    return keep * value + up * turned(value, -1) - low * turned(value, 1)


def sides_kernel(left_ref, right_ref, west_ref, east_ref, coef_out):
    def sources(i, carry):
        for k in range(CHUNK):
            s = i * CHUNK + k
            for half in range(HALVES):
                strips = fill_halo(left_ref[s, half], right_ref[s, half], west_ref[s, half], east_ref[s, half])
                for side in range(2):
                    for n, value in enumerate(stencil_of(strips[side])):
                        coef_out[s, half, side, n] = value
        return carry

    lax.fori_loop(0, BANDS // CHUNK, sources, 0)


def mix_kernel(
    kern_ref, cols_ref, field_ref, cy_ref, before_ref, after_ref, diff_hbm, conv_hbm, base_hbm, top_hbm,
    keep_out, give_out, far_out,
    parts, onehot, added, mixed, diff_buf, conv_ref, base_ref, top_ref, diff_sem, sem,
):
    def diff_copy(g):
        span = pl.ds(g * GROUP, GROUP)
        return pltpu.make_async_copy(diff_hbm.at[span], diff_buf.at[span], diff_sem.at[g])

    small = [
        pltpu.make_async_copy(conv_hbm, conv_ref, sem.at[0]),
        pltpu.make_async_copy(base_hbm, base_ref, sem.at[1]),
        pltpu.make_async_copy(top_hbm, top_ref, sem.at[2]),
    ]
    for copy in small + [diff_copy(g) for g in range(ROWS // GROUP)]:
        copy.start()
    for c in range(8):
        span = slice(c * 128, c * 128 + 128)
        hi, lo = split(kern_ref[span, :])
        parts[span, :LEV] = hi
        parts[span, LEV:] = lo

    for copy in small:
        copy.wait()
    level = lax.broadcasted_iota(jnp.int32, (LEV, LON), 0)

    half = parts.shape[0] // 2

    def spread(g):
        cols = cols_ref[...]
        for q in range(GROUP):
            here = jnp.where(cols // LON == g * GROUP + q, cols % LON, -1).astype(f32).astype(bf16)
            for r in range(0, LON, 32):
                cell = lax.broadcasted_iota(jnp.int32, (32, cols.shape[1]), 0) + r
                match = cell.astype(f32).astype(bf16) == here
                onehot[g, q * LON + r : q * LON + r + 32, :] = jnp.where(
                    match, jnp.ones((), bf16), jnp.zeros((), bf16)
                )
        first = jnp.dot(onehot[g, :, :half], parts[:half], preferred_element_type=f32)
        second = jnp.dot(onehot[g, :, half:], parts[half:], preferred_element_type=f32)
        both = first + second
        added[g] = both[:, :LEV] + both[:, LEV:]

    def column(g):
        diff_copy(g).wait()
        for q in range(GROUP):
            row = g * GROUP + q
            forced = field_ref[row] + added[g, q * LON : (q + 1) * LON].T
            base = base_ref[row : row + 1, :]
            top = top_ref[row : row + 1, :]
            inside = jnp.where((level >= base) & (level <= top), 1.0, 0.0)
            mean = jnp.sum(inside * forced, axis=0, keepdims=True) / (top - base + 1).astype(f32)
            convected = forced + conv_ref[row : row + 1, :] * inside * (mean - forced)
            hi, lo = split(convected)
            pair = jnp.concatenate([hi, lo], axis=1)
            both = jnp.dot(diff_buf[row], jnp.concatenate([pair, pair], axis=0), preferred_element_type=f32)
            mixed[row] = both[:, :LON] + both[:, LON:]

    spread(0)
    for g in range(ROWS // GROUP):
        if g + 1 < ROWS // GROUP:
            spread(g + 1)
        column(g)

    open_face = jnp.where(lax.axis_index("band") == BANDS - 1, 0.0, 1.0)
    z, core = lax.axis_index("band") // CORES, lax.axis_index("band") % CORES

    def meridional(slab, store):
        span = pl.ds(pl.multiple_of(slab * SLAB, SLAB), SLAB)
        faces = {}

        def face(row):
            if row not in faces:
                if row < 0:
                    courant = before_ref[row + 2, span]
                elif row == ROWS:
                    courant = after_ref[0, span]
                else:
                    courant = cy_ref[row, span]
                if row == ROWS - 1:
                    courant = courant * open_face
                faces[row] = jnp.maximum(courant, 0.0), jnp.minimum(courant, 0.0)
            return faces[row]

        def partial_sweep(values, row):
            terms = []
            if row in values:
                terms.append((1.0 - face(row)[0] + face(row - 1)[1]) * values[row])
            if row + 1 in values:
                terms.append(face(row)[0] * values[row + 1])
            if row - 1 in values:
                terms.append(-(face(row - 1)[1] * values[row - 1]))
            return sum(terms[1:], terms[0])

        values = {row: mixed[row, span] for row in range(ROWS)}
        swept = {-1: partial_sweep(values, -1)}
        for row in range(ROWS + 4):
            if row <= ROWS:
                swept[row] = partial_sweep(values, row)
            store(row - 2, partial_sweep(swept, row - 2))

    for t in range(CHIPS):
        pair = CORES * ((z + t) % CHIPS)

        def keep(row, value):
            keep_out[t, row + 2] = value
            if t == FAR:
                far_out[row + 2] = value

        def give(row, value):
            give_out[t, row + 2] = value

        meridional(pair + core, keep)
        meridional(pair + 1 - core, give)


def join_kernel(keep_ref, got_ref, *outs):
    core = lax.axis_index("band") % CORES

    def join(south, north):
        for out, t in zip(outs[1:], NEAR):
            out[0 : ROWS + 2] = south[t, 0 : ROWS + 2]
            out[ROWS + 2 :] = north[t, 2:]
            out[ROWS : ROWS + 2] += north[t, 0:2]
            out[ROWS + 2 : ROWS + 4] += south[t, ROWS + 2 :]

    outs[0][...] = got_ref[FAR]
    pl.when(core == 0)(lambda: join(keep_ref, got_ref))
    pl.when(core == 1)(lambda: join(got_ref, keep_ref))


def pack_kernel(*refs):
    moved, (own_out, left_out, right_out) = refs[: CHIPS + 1], refs[CHIPS + 1 :]
    z, core = lax.axis_index("band") // CORES, lax.axis_index("band") % CORES
    far = (z - FAR) % CHIPS * CORES
    blocks = [(moved[0], far + core, 1), (moved[1], far + 1 - core, 1)]
    blocks += [(ref, (z - t) % CHIPS * CORES, CORES) for ref, t in zip(moved[2:], NEAR)]
    for ref, s, n in blocks:
        own_out[pl.ds(s * ROWS, n * ROWS)] = ref[2 : n * ROWS + 2]
    for ref, s, n in blocks:
        south = pl.ds(jnp.maximum(s - 1, 0) * ROWS + ROWS - 2, 2)
        own_out[south] += jnp.where(s > 0, ref[0:2], 0.0)
        north = pl.ds(jnp.minimum(s + n, BANDS - 1) * ROWS, 2)
        own_out[north] += jnp.where(s + n < BANDS, ref[n * ROWS + 2 :], 0.0)

    def pack(i, carry):
        for k in range(CHUNK):
            s = i * CHUNK + k
            left, right = pack_strips(lambda row: own_out[s * ROWS + row])
            for half in range(HALVES):
                left_out[s, half] = left[half]
                right_out[s, half] = right[half]
        return carry

    lax.fori_loop(0, BANDS // CHUNK, pack, 0)


def zonal_kernel(part, own_ref, cx_ref, low_ref, out_ref, first, second):
    tiles = CHUNK * ROWS
    chunks = BANDS // CHUNK // 2

    def sources(i, carry):
        old, new = first, second
        for step in range(XSTEPS):
            for t in range(tiles):
                value = own_ref[(part * chunks + i) * tiles + t] if step == 0 else old[t]
                up = jnp.maximum(cx_ref[(part * chunks + i) * tiles + t], 0.0)
                low = low_ref[(part * chunks + i) * tiles + t]
                value = zonal_sweep(value, 1.0 - up + low, up, low)
                if step == XSTEPS - 1:
                    out_ref[i * tiles + t] = value
                else:
                    new[t] = value
            old, new = new, old
        return carry

    lax.fori_loop(0, chunks, sources, 0)


def merge_kernel(inner_a, inner_b, left_ref, right_ref, west_ref, east_ref, coef_ref, out_hbm, sides, left_buf, right_buf, out_ref, sem):
    count = BANDS * HALVES
    for n in range(count):
        s, half = n // HALVES, n % HALVES
        left_buf[n], right_buf[n] = fill_halo(
            left_ref[s, half], right_ref[s, half], west_ref[s, half], east_ref[s, half]
        )
    for _ in range(XSTEPS):
        for n in range(count):
            s, half = n // HALVES, n % HALVES
            for side, buf in enumerate((left_buf, right_buf)):
                buf[n] = zonal_sweep(buf[n], *(coef_ref[s, half, side, k] for k in range(3)))
    spot = lane_iota((SLAB, LON)) % STRIP
    for n in range(count):
        sides[n] = jnp.where(spot < XSTEPS, turned(right_buf[n], -2 * XSTEPS), left_buf[n])
    lane = lane_iota((SLAB, LON))
    outer = (lane < XSTEPS) | (lane >= LON - XSTEPS)

    def store(c):
        span = pl.ds(c * CHUNK * ROWS, CHUNK * ROWS)
        return pltpu.make_async_copy(out_ref.at[:, span], out_hbm.at[:, span], sem.at[c])

    for c in range(BANDS // CHUNK):
        for i in range(c * CHUNK, c * CHUNK + CHUNK):
            for k in range(HALVES):
                packed = sides[i * HALVES + k]
                for g in range(ROWS // HALVES):
                    lat = i * ROWS + k * (ROWS // HALVES) + g
                    inner = inner_a[lat] if i < BANDS // 2 else inner_b[lat - BANDS // 2 * ROWS]
                    out_ref[:, lat, :] = jnp.where(outer, turned(packed, -STRIP * g - XSTEPS), inner)
        store(c).start()
    for c in range(BANDS // CHUNK):
        store(c).wait()


def call(body, outs, args, scratch=(), hbm_in=(), hbm_out=(), vmem=16):
    def place(k, far):
        return pl.BlockSpec(memory_space=pltpu.HBM if k in far else pltpu.VMEM)

    args = [pltpu.with_memory_space_constraint(x, pltpu.HBM) if k in hbm_in else x for k, x in enumerate(args)]
    return pl.pallas_call(
        body,
        out_shape=[
            (pltpu.HBM if k in hbm_out else jax.ShapeDtypeStruct)(shape, kind) for k, (shape, kind) in enumerate(outs)
        ],
        in_specs=[place(k, hbm_in) for k in range(len(args))],
        out_specs=[place(k, hbm_out) for k in range(len(outs))],
        scratch_shapes=list(scratch),
        compiler_params=pltpu.CompilerParams(vmem_limit_bytes=vmem << 20),
    )(*args)


def ring_pair(up_value, down_value, axis, wrap):
    n = lax.axis_size(axis)
    up = [(i, (i + 1) % n) for i in range(n if wrap else n - 1)]
    from_prev = lax.ppermute(up_value, axis, up)
    from_next = lax.ppermute(down_value, axis, [(b, a) for a, b in up])
    return from_prev, from_next


def swap_bands(blocks):
    return lax.all_to_all(blocks, "band", split_axis=0, concat_axis=0, tiled=True)


def step_adjoint(
    adjoint_in, courant_y, courant_x, diffusion_inverse, conv_weight, cloud_base, cloud_top,
    sound_count, xco2_adjoint, kernel, sound_cols,
):
    slots = kernel.shape[2]
    dma = pltpu.SemaphoreType.DMA
    (kern,) = call(
        scale_kernel,
        [(kernel.shape[1:], f32)],
        (sound_count, xco2_adjoint, kernel),
        (
            pltpu.VMEM(sound_count.shape, jnp.int32),
            pltpu.VMEM(xco2_adjoint.shape, f32),
            pltpu.VMEM(kernel.shape[1:], f32),
            dma((2,)),
            dma((BANDS // GROUP,)),
        ),
        hbm_in=(0, 1, 2),
    )
    kern = swap_bands(kern)

    grid = (ROWS, LEV, LON)
    field, cy, diff = call(
        prepare_kernel,
        [(grid, f32), (grid, f32), ((ROWS, LEV, 2 * LEV), bf16)],
        (adjoint_in, courant_y, diffusion_inverse),
        (
            pltpu.VMEM(adjoint_in.shape, f32),
            pltpu.VMEM(courant_y.shape, f32),
            pltpu.VMEM(diffusion_inverse.shape, f32),
            pltpu.VMEM((ROWS, LEV, 2 * LEV), bf16),
            dma((3,)),
            dma,
        ),
        hbm_in=(0, 1, 2),
        hbm_out=(2,),
    )
    cy_before, cy_after = ring_pair(cy[ROWS - 2 :], cy[:1], "band", False)

    keep, give, far = call(
        mix_kernel,
        [((CHIPS, WIDE, SLAB, LON), f32)] * 2 + [((WIDE, SLAB, LON), f32)],
        (
            kern.reshape(BANDS * slots, LEV),
            sound_cols.reshape(1, BANDS * slots),
            field,
            cy,
            cy_before,
            cy_after,
            diff,
            conv_weight,
            cloud_base,
            cloud_top,
        ),
        (
            pltpu.VMEM((BANDS * slots, 2 * LEV), bf16),
            pltpu.VMEM((ROWS // GROUP, GROUP * LON, BANDS * slots), bf16),
            pltpu.VMEM((ROWS // GROUP, GROUP * LON, LEV), f32),
            pltpu.VMEM(grid, f32),
            pltpu.VMEM((ROWS, LEV, 2 * LEV), bf16),
            pltpu.VMEM((ROWS, LON), f32),
            pltpu.VMEM((ROWS, LON), jnp.int32),
            pltpu.VMEM((ROWS, LON), jnp.int32),
            dma((ROWS // GROUP,)),
            dma((3,)),
        ),
        hbm_in=(6, 7, 8, 9),
        vmem=24,
    )
    got = lax.ppermute(give, "band", [(i, i ^ 1) for i in range(BANDS)])

    def move(block, t):
        return lax.ppermute(block, "band", [(i, (i + CORES * t) % BANDS) for i in range(BANDS)])

    far = move(far, FAR)
    rest, *near = call(
        join_kernel,
        [((WIDE, SLAB, LON), f32)] + [((ROWS + WIDE, SLAB, LON), f32)] * len(NEAR),
        (keep, got),
    )
    near = [near[0]] + [move(block, t) for block, t in zip(near[1:], NEAR[1:])]
    moved = (far, move(rest, FAR), *near)

    strips = (BANDS, HALVES, SLAB, LON)
    tiles = (BANDS * ROWS, SLAB, LON)
    cx, cx_low, cx_left, cx_right = call(faces_kernel, [(tiles, f32), (tiles, f32), (strips, f32), (strips, f32)], (courant_x,))
    cx_west, cx_east = ring_pair(cx_right, cx_left, "region", True)
    (coef,) = call(
        sides_kernel,
        [((BANDS, HALVES, 2, 3, SLAB, LON), f32)],
        (cx_left, cx_right, cx_west, cx_east),
    )
    own, left, right = call(pack_kernel, [(tiles, f32), (strips, f32), (strips, f32)], moved)
    regions = lax.axis_size("region")
    west = lax.ppermute(right, "region", [(i, (i + 1) % regions) for i in range(regions)])
    east = lax.ppermute(left, "region", [((i + 1) % regions, i) for i in range(regions)])
    chunk = pltpu.VMEM((CHUNK * ROWS, SLAB, LON), f32)
    inner = []
    for part in range(2):
        inner += call(
            functools.partial(zonal_kernel, part),
            [((BANDS * ROWS // 2, SLAB, LON), f32)],
            (own, cx, cx_low),
            (chunk,) * 2,
        )
    flat = pltpu.VMEM((BANDS * HALVES, SLAB, LON), f32)
    return call(
        merge_kernel,
        [((SLAB, BANDS * ROWS, LON), f32)],
        (*inner, left, right, west, east, coef),
        (flat,) * 3 + (pltpu.VMEM((SLAB, BANDS * ROWS, LON), f32), dma((BANDS // CHUNK,))),
        hbm_out=(0,),
    )[0]


def solution(mesh):
    in_specs = (
        P(None, "band", "region"),
        P(None, "band", "region"),
        P("band", None, "region"),
        P("band", None, None),
        P("band", "region"),
        P("band", "region"),
        P("band", "region"),
        P("region", "band"),
        P("region", "band", None),
        P("region", "band", None, None),
        P("region", "band", None),
    )
    out_specs = P("band", None, "region")
    return jax.shard_map(
        step_adjoint, mesh=mesh, in_specs=in_specs, out_specs=out_specs, check_vma=False
    )
```

```python
import jax
import jax.numpy as jnp
from jax import lax
from jax.experimental import pallas as pl
from jax.experimental.pallas import tpu as pltpu
from jax.sharding import PartitionSpec as P


XSTEPS = 4
LEV = 128
ROWS = 16
LON = 128
BANDS = 16
SLAB = 8
STRIP = 16
HALVES = 2
GROUP = 4
CHUNK = 4
CORES = 2
CHIPS = BANDS // CORES
FAR = CHIPS // 2
NEAR = (0, 3, 5, 2, 6, 1, 7)
WIDE = ROWS + 4

f32 = jnp.float32
bf16 = jnp.bfloat16


def split(x):
    hi = x.astype(bf16)
    return hi, (x - hi.astype(f32)).astype(bf16)


def lane_iota(shape):
    return lax.broadcasted_iota(jnp.int32, shape, len(shape) - 1)


def turned(x, shift):
    shift %= LON
    return pltpu.roll(x, shift, x.ndim - 1) if shift else x


def pack_strips(tile_of):
    left, right = [], []
    for half in range(HALVES):
        west = east = None
        for g in range(ROWS // HALVES):
            tile = tile_of(half * (ROWS // HALVES) + g)
            here = lane_iota(tile.shape) // STRIP == g
            to_west = turned(tile, STRIP * g + XSTEPS)
            to_east = turned(tile, STRIP * g + STRIP - XSTEPS)
            west = to_west if west is None else jnp.where(here, to_west, west)
            east = to_east if east is None else jnp.where(here, to_east, east)
        left.append(west)
        right.append(east)
    return left, right


def scale_kernel(count_hbm, value_hbm, kern_hbm, out_ref, count, value, kern, sem, kern_sem):
    small = [
        pltpu.make_async_copy(count_hbm, count, sem.at[0]),
        pltpu.make_async_copy(value_hbm, value, sem.at[1]),
    ]
    spans = [pl.ds(c * GROUP, GROUP) for c in range(BANDS // GROUP)]
    loads = [pltpu.make_async_copy(kern_hbm.at[0, spans[c]], kern.at[spans[c]], kern_sem.at[c]) for c in range(len(spans))]
    for copy in small + loads:
        copy.start()
    for copy in small:
        copy.wait()
    factor = value[0].T
    live = lax.broadcasted_iota(jnp.int32, factor.shape, 0) < count[...]
    factor = jnp.where(live, factor, 0.0)
    for c in range(len(spans)):
        loads[c].wait()
        for band in range(c * GROUP, c * GROUP + GROUP):
            out_ref[band] = kern[band] * factor[:, band : band + 1]


def prepare_kernel(field_hbm, cy_hbm, diff_hbm, field_out, cy_out, diff_out, field, cy, diff, parts, sem, out_sem):
    loads = [
        pltpu.make_async_copy(diff_hbm, diff, sem.at[0]),
        pltpu.make_async_copy(field_hbm, field, sem.at[1]),
        pltpu.make_async_copy(cy_hbm, cy, sem.at[2]),
    ]
    for copy in loads:
        copy.start()
    loads[0].wait()
    for row in range(ROWS):
        hi, lo = split(diff[row].T)
        parts[row, :, :LEV] = hi
        parts[row, :, LEV:] = lo
    store = pltpu.make_async_copy(parts, diff_out, out_sem)
    store.start()
    loads[1].wait()
    for row in range(ROWS):
        field_out[row] = field[:, row, :]
    loads[2].wait()
    for row in range(ROWS):
        cy_out[row] = cy[:, row, :]
    store.wait()


def faces_kernel(cx_ref, cx_out, low_out, left_out, right_out):
    def sources(i, carry):
        for k in range(2):
            s = i * 2 + k

            def tile_of(row):
                tile = cx_ref[:, pl.ds(s * ROWS + row, 1), :].reshape(SLAB, LON)
                cx_out[s * ROWS + row] = tile
                low_out[s * ROWS + row] = turned(jnp.minimum(tile, 0.0), 1)
                return tile

            left, right = pack_strips(tile_of)
            for half in range(HALVES):
                left_out[s, half] = left[half]
                right_out[s, half] = right[half]
        return carry

    lax.fori_loop(0, BANDS // 2, sources, 0)


def fill_halo(left, right, west, east):
    spot = lane_iota(left.shape) % STRIP
    left = jnp.where(spot < XSTEPS, turned(west, XSTEPS - STRIP + XSTEPS), left)
    right = jnp.where(spot >= STRIP - XSTEPS, turned(east, STRIP - 2 * XSTEPS), right)
    return left, right


def stencil_of(courant):
    up = jnp.maximum(courant, 0.0)
    low = turned(jnp.minimum(courant, 0.0), 1)
    return 1.0 - up + low, up, low


def zonal_sweep(value, keep, up, low):
    return keep * value + up * turned(value, -1) - low * turned(value, 1)


def sides_kernel(left_ref, right_ref, west_ref, east_ref, coef_out):
    def sources(i, carry):
        for k in range(CHUNK):
            s = i * CHUNK + k
            for half in range(HALVES):
                strips = fill_halo(left_ref[s, half], right_ref[s, half], west_ref[s, half], east_ref[s, half])
                for side in range(2):
                    for n, value in enumerate(stencil_of(strips[side])):
                        coef_out[s, half, side, n] = value
        return carry

    lax.fori_loop(0, BANDS // CHUNK, sources, 0)


def mix_kernel(
    kern_ref, cols_ref, field_ref, cy_ref, before_ref, after_ref, diff_hbm, conv_hbm, base_hbm, top_hbm,
    keep_out, give_out, far_out,
    parts, onehot, added, mixed, diff_buf, conv_ref, base_ref, top_ref, diff_sem, sem,
):
    def diff_copy(g):
        span = pl.ds(g * GROUP, GROUP)
        return pltpu.make_async_copy(diff_hbm.at[span], diff_buf.at[span], diff_sem.at[g])

    small = [
        pltpu.make_async_copy(conv_hbm, conv_ref, sem.at[0]),
        pltpu.make_async_copy(base_hbm, base_ref, sem.at[1]),
        pltpu.make_async_copy(top_hbm, top_ref, sem.at[2]),
    ]
    for copy in small + [diff_copy(g) for g in range(ROWS // GROUP)]:
        copy.start()
    for c in range(8):
        span = slice(c * 128, c * 128 + 128)
        hi, lo = split(kern_ref[span, :])
        parts[span, :LEV] = hi
        parts[span, LEV:] = lo

    for copy in small:
        copy.wait()
    level = lax.broadcasted_iota(jnp.int32, (LEV, LON), 0)

    half = parts.shape[0] // 2

    def spread(g):
        cols = cols_ref[...]
        for q in range(GROUP):
            here = jnp.where(cols // LON == g * GROUP + q, cols % LON, -1).astype(f32).astype(bf16)
            for r in range(0, LON, 32):
                cell = lax.broadcasted_iota(jnp.int32, (32, cols.shape[1]), 0) + r
                match = cell.astype(f32).astype(bf16) == here
                onehot[g, q * LON + r : q * LON + r + 32, :] = jnp.where(
                    match, jnp.ones((), bf16), jnp.zeros((), bf16)
                )
        first = jnp.dot(onehot[g, :, :half], parts[:half], preferred_element_type=f32)
        second = jnp.dot(onehot[g, :, half:], parts[half:], preferred_element_type=f32)
        both = first + second
        added[g] = both[:, :LEV] + both[:, LEV:]

    def column(g):
        diff_copy(g).wait()
        for q in range(GROUP):
            row = g * GROUP + q
            forced = field_ref[row] + added[g, q * LON : (q + 1) * LON].T
            base = base_ref[row : row + 1, :]
            top = top_ref[row : row + 1, :]
            inside = jnp.where((level >= base) & (level <= top), 1.0, 0.0)
            mean = jnp.sum(inside * forced, axis=0, keepdims=True) / (top - base + 1).astype(f32)
            convected = forced + conv_ref[row : row + 1, :] * inside * (mean - forced)
            hi, lo = split(convected)
            pair = jnp.concatenate([hi, lo], axis=1)
            both = jnp.dot(diff_buf[row], jnp.concatenate([pair, pair], axis=0), preferred_element_type=f32)
            mixed[row] = both[:, :LON] + both[:, LON:]

    spread(0)
    for g in range(ROWS // GROUP):
        if g + 1 < ROWS // GROUP:
            spread(g + 1)
        column(g)

    open_face = jnp.where(lax.axis_index("band") == BANDS - 1, 0.0, 1.0)
    z, core = lax.axis_index("band") // CORES, lax.axis_index("band") % CORES

    def meridional(slab, store):
        span = pl.ds(pl.multiple_of(slab * SLAB, SLAB), SLAB)
        faces = {}

        def face(row):
            if row not in faces:
                if row < 0:
                    courant = before_ref[row + 2, span]
                elif row == ROWS:
                    courant = after_ref[0, span]
                else:
                    courant = cy_ref[row, span]
                if row == ROWS - 1:
                    courant = courant * open_face
                faces[row] = jnp.maximum(courant, 0.0), jnp.minimum(courant, 0.0)
            return faces[row]

        def partial_sweep(values, row):
            terms = []
            if row in values:
                terms.append((1.0 - face(row)[0] + face(row - 1)[1]) * values[row])
            if row + 1 in values:
                terms.append(face(row)[0] * values[row + 1])
            if row - 1 in values:
                terms.append(-(face(row - 1)[1] * values[row - 1]))
            return sum(terms[1:], terms[0])

        values = {row: mixed[row, span] for row in range(ROWS)}
        swept = {-1: partial_sweep(values, -1)}
        for row in range(ROWS + 4):
            if row <= ROWS:
                swept[row] = partial_sweep(values, row)
            store(row - 2, partial_sweep(swept, row - 2))

    for t in range(CHIPS):
        pair = CORES * ((z + t) % CHIPS)

        def keep(row, value):
            keep_out[t, row + 2] = value
            if t == FAR:
                far_out[row + 2] = value

        def give(row, value):
            give_out[t, row + 2] = value

        meridional(pair + core, keep)
        meridional(pair + 1 - core, give)


def join_kernel(keep_ref, got_ref, *outs):
    core = lax.axis_index("band") % CORES

    def join(south, north):
        for out, t in zip(outs[1:], NEAR):
            out[0 : ROWS + 2] = south[t, 0 : ROWS + 2]
            out[ROWS + 2 :] = north[t, 2:]
            out[ROWS : ROWS + 2] += north[t, 0:2]
            out[ROWS + 2 : ROWS + 4] += south[t, ROWS + 2 :]

    outs[0][...] = got_ref[FAR]
    pl.when(core == 0)(lambda: join(keep_ref, got_ref))
    pl.when(core == 1)(lambda: join(got_ref, keep_ref))


def pack_kernel(*refs):
    moved, (own_out, left_out, right_out) = refs[: CHIPS + 1], refs[CHIPS + 1 :]
    z, core = lax.axis_index("band") // CORES, lax.axis_index("band") % CORES
    far = (z - FAR) % CHIPS * CORES
    blocks = [(moved[0], far + core, 1), (moved[1], far + 1 - core, 1)]
    blocks += [(ref, (z - t) % CHIPS * CORES, CORES) for ref, t in zip(moved[2:], NEAR)]
    for ref, s, n in blocks:
        own_out[pl.ds(s * ROWS, n * ROWS)] = ref[2 : n * ROWS + 2]
    for ref, s, n in blocks:
        south = pl.ds(jnp.maximum(s - 1, 0) * ROWS + ROWS - 2, 2)
        own_out[south] += jnp.where(s > 0, ref[0:2], 0.0)
        north = pl.ds(jnp.minimum(s + n, BANDS - 1) * ROWS, 2)
        own_out[north] += jnp.where(s + n < BANDS, ref[n * ROWS + 2 :], 0.0)

    def pack(i, carry):
        for k in range(CHUNK):
            s = i * CHUNK + k
            left, right = pack_strips(lambda row: own_out[s * ROWS + row])
            for half in range(HALVES):
                left_out[s, half] = left[half]
                right_out[s, half] = right[half]
        return carry

    lax.fori_loop(0, BANDS // CHUNK, pack, 0)


def zonal_kernel(own_ref, cx_ref, low_ref, out_ref, first, second):
    tiles = CHUNK * ROWS

    def sources(i, carry):
        old, new = first, second
        for step in range(XSTEPS):
            for t in range(tiles):
                value = own_ref[i * tiles + t] if step == 0 else old[t]
                up = jnp.maximum(cx_ref[i * tiles + t], 0.0)
                low = low_ref[i * tiles + t]
                value = zonal_sweep(value, 1.0 - up + low, up, low)
                if step == XSTEPS - 1:
                    out_ref[i * tiles + t] = value
                else:
                    new[t] = value
            old, new = new, old
        return carry

    lax.fori_loop(0, BANDS // CHUNK, sources, 0)


def merge_kernel(inner_ref, left_ref, right_ref, west_ref, east_ref, coef_ref, out_hbm, sides, left_buf, right_buf, out_ref, sem):
    count = BANDS * HALVES
    for n in range(count):
        s, half = n // HALVES, n % HALVES
        left_buf[n], right_buf[n] = fill_halo(
            left_ref[s, half], right_ref[s, half], west_ref[s, half], east_ref[s, half]
        )
    for _ in range(XSTEPS):
        for n in range(count):
            s, half = n // HALVES, n % HALVES
            for side, buf in enumerate((left_buf, right_buf)):
                buf[n] = zonal_sweep(buf[n], *(coef_ref[s, half, side, k] for k in range(3)))
    spot = lane_iota((SLAB, LON)) % STRIP
    for n in range(count):
        sides[n] = jnp.where(spot < XSTEPS, turned(right_buf[n], -2 * XSTEPS), left_buf[n])
    lane = lane_iota((SLAB, LON))
    outer = (lane < XSTEPS) | (lane >= LON - XSTEPS)

    def store(c):
        span = pl.ds(c * CHUNK * ROWS, CHUNK * ROWS)
        return pltpu.make_async_copy(out_ref.at[:, span], out_hbm.at[:, span], sem.at[c])

    for c in range(BANDS // CHUNK):
        for i in range(c * CHUNK, c * CHUNK + CHUNK):
            for k in range(HALVES):
                packed = sides[i * HALVES + k]
                for g in range(ROWS // HALVES):
                    lat = i * ROWS + k * (ROWS // HALVES) + g
                    out_ref[:, lat, :] = jnp.where(outer, turned(packed, -STRIP * g - XSTEPS), inner_ref[lat])
        store(c).start()
    for c in range(BANDS // CHUNK):
        store(c).wait()


def call(body, outs, args, scratch=(), hbm_in=(), hbm_out=(), vmem=16):
    def place(k, far):
        return pl.BlockSpec(memory_space=pltpu.HBM if k in far else pltpu.VMEM)

    args = [pltpu.with_memory_space_constraint(x, pltpu.HBM) if k in hbm_in else x for k, x in enumerate(args)]
    return pl.pallas_call(
        body,
        out_shape=[
            (pltpu.HBM if k in hbm_out else jax.ShapeDtypeStruct)(shape, kind) for k, (shape, kind) in enumerate(outs)
        ],
        in_specs=[place(k, hbm_in) for k in range(len(args))],
        out_specs=[place(k, hbm_out) for k in range(len(outs))],
        scratch_shapes=list(scratch),
        compiler_params=pltpu.CompilerParams(vmem_limit_bytes=vmem << 20),
    )(*args)


def ring_pair(up_value, down_value, axis, wrap):
    n = lax.axis_size(axis)
    up = [(i, (i + 1) % n) for i in range(n if wrap else n - 1)]
    from_prev = lax.ppermute(up_value, axis, up)
    from_next = lax.ppermute(down_value, axis, [(b, a) for a, b in up])
    return from_prev, from_next


def swap_bands(blocks):
    return lax.all_to_all(blocks, "band", split_axis=0, concat_axis=0, tiled=True)


def step_adjoint(
    adjoint_in, courant_y, courant_x, diffusion_inverse, conv_weight, cloud_base, cloud_top,
    sound_count, xco2_adjoint, kernel, sound_cols,
):
    slots = kernel.shape[2]
    dma = pltpu.SemaphoreType.DMA
    (kern,) = call(
        scale_kernel,
        [(kernel.shape[1:], f32)],
        (sound_count, xco2_adjoint, kernel),
        (
            pltpu.VMEM(sound_count.shape, jnp.int32),
            pltpu.VMEM(xco2_adjoint.shape, f32),
            pltpu.VMEM(kernel.shape[1:], f32),
            dma((2,)),
            dma((BANDS // GROUP,)),
        ),
        hbm_in=(0, 1, 2),
    )
    kern = swap_bands(kern)

    grid = (ROWS, LEV, LON)
    field, cy, diff = call(
        prepare_kernel,
        [(grid, f32), (grid, f32), ((ROWS, LEV, 2 * LEV), bf16)],
        (adjoint_in, courant_y, diffusion_inverse),
        (
            pltpu.VMEM(adjoint_in.shape, f32),
            pltpu.VMEM(courant_y.shape, f32),
            pltpu.VMEM(diffusion_inverse.shape, f32),
            pltpu.VMEM((ROWS, LEV, 2 * LEV), bf16),
            dma((3,)),
            dma,
        ),
        hbm_in=(0, 1, 2),
        hbm_out=(2,),
    )
    cy_before, cy_after = ring_pair(cy[ROWS - 2 :], cy[:1], "band", False)

    keep, give, far = call(
        mix_kernel,
        [((CHIPS, WIDE, SLAB, LON), f32)] * 2 + [((WIDE, SLAB, LON), f32)],
        (
            kern.reshape(BANDS * slots, LEV),
            sound_cols.reshape(1, BANDS * slots),
            field,
            cy,
            cy_before,
            cy_after,
            diff,
            conv_weight,
            cloud_base,
            cloud_top,
        ),
        (
            pltpu.VMEM((BANDS * slots, 2 * LEV), bf16),
            pltpu.VMEM((ROWS // GROUP, GROUP * LON, BANDS * slots), bf16),
            pltpu.VMEM((ROWS // GROUP, GROUP * LON, LEV), f32),
            pltpu.VMEM(grid, f32),
            pltpu.VMEM((ROWS, LEV, 2 * LEV), bf16),
            pltpu.VMEM((ROWS, LON), f32),
            pltpu.VMEM((ROWS, LON), jnp.int32),
            pltpu.VMEM((ROWS, LON), jnp.int32),
            dma((ROWS // GROUP,)),
            dma((3,)),
        ),
        hbm_in=(6, 7, 8, 9),
        vmem=24,
    )
    got = lax.ppermute(give, "band", [(i, i ^ 1) for i in range(BANDS)])

    def move(block, t):
        return lax.ppermute(block, "band", [(i, (i + CORES * t) % BANDS) for i in range(BANDS)])

    far = move(far, FAR)
    rest, *near = call(
        join_kernel,
        [((WIDE, SLAB, LON), f32)] + [((ROWS + WIDE, SLAB, LON), f32)] * len(NEAR),
        (keep, got),
    )
    near = [near[0]] + [move(block, t) for block, t in zip(near[1:], NEAR[1:])]
    moved = (far, move(rest, FAR), *near)

    strips = (BANDS, HALVES, SLAB, LON)
    tiles = (BANDS * ROWS, SLAB, LON)
    cx, cx_low, cx_left, cx_right = call(faces_kernel, [(tiles, f32), (tiles, f32), (strips, f32), (strips, f32)], (courant_x,))
    cx_west, cx_east = ring_pair(cx_right, cx_left, "region", True)
    (coef,) = call(
        sides_kernel,
        [((BANDS, HALVES, 2, 3, SLAB, LON), f32)],
        (cx_left, cx_right, cx_west, cx_east),
    )
    own, left, right = call(pack_kernel, [(tiles, f32), (strips, f32), (strips, f32)], moved)
    west, east = ring_pair(right, left, "region", True)
    chunk = pltpu.VMEM((CHUNK * ROWS, SLAB, LON), f32)
    (inner,) = call(zonal_kernel, [(tiles, f32)], (own, cx, cx_low), (chunk,) * 2)
    flat = pltpu.VMEM((BANDS * HALVES, SLAB, LON), f32)
    return call(
        merge_kernel,
        [((SLAB, BANDS * ROWS, LON), f32)],
        (inner, left, right, west, east, coef),
        (flat,) * 3 + (pltpu.VMEM((SLAB, BANDS * ROWS, LON), f32), dma((BANDS // CHUNK,))),
        hbm_out=(0,),
    )[0]


def solution(mesh):
    in_specs = (
        P(None, "band", "region"),
        P(None, "band", "region"),
        P("band", None, "region"),
        P("band", None, None),
        P("band", "region"),
        P("band", "region"),
        P("band", "region"),
        P("region", "band"),
        P("region", "band", None),
        P("region", "band", None, None),
        P("region", "band", None),
    )
    out_specs = P("band", None, "region")
    return jax.shard_map(step_adjoint, mesh=mesh, in_specs=in_specs, out_specs=out_specs, check_vma=False)
```
